32 devices in a mesh: section: 4 (over x, core), dp: 8 (over z, y).
Axes of the slice: x: 2, y: 2, z: 4, core: 2. Of those that a mesh axis runs over, the one named last changes fastest.
Arguments:
- text_ids: int32 [24, 77], P('dp'), may hold values from 0 to 12351
- seed_ids: int32 [24], P('dp'), may hold values from 0 to 1023
- text_table: bfloat16 [12352, 512], P('dp'), may hold values from -16 to 16
- latent_table: float32 [1024, 512], replicated, may hold values from -6 to 6
- start_map: bfloat16 [512, 256], replicated, may hold values from -6 to 6
- style_weight: bfloat16 [4, 512, 512], P('section'), may hold values from -0.25 to 0.25
- conv_weight: bfloat16 [4, 512, 9, 512], P('section'), may hold values from -1 to 1
- score_head: float32 [512], replicated, may hold values from -6 to 6
Outputs:
- conv_grad: float32 [4, 512, 9, 512], P('section', 'dp')
The draws below stay inside these ranges and needn't reach their ends.
All inputs are finite; a program needn't handle non-finite values.
Results may differ from the reference program's by a relative error of at most 0.01.
Values may be sent and summed in bfloat16 or wider, within the bound.
No kernel may reach another device: no remote copies, remote signals or barrier semaphores. Data moves between devices by JAX's collectives and lax.ppermute only.
A program may use at most 128 MiB of HBM per device.

```python
import math
from functools import partial
import jax
import jax.numpy as jnp
import numpy as np
from jax import lax

C = 512
RES = 16
ZD = 512
TXT_LEN = 77
SEEDS = 1024
BATCH = 24
VOCAB = 12352
GEN_SECTIONS = 3
N_SECTION = 4


def draw_conv_weight(key, part):
    base_key = jax.random.fold_in(key, 11)
    first_key, second_key, third_key = jax.random.split(base_key, 3)
    shape = (N_SECTION, C, 9, C)
    base = jax.random.normal(first_key, shape, jnp.float32)
    row_scale = jnp.exp(jax.random.uniform(second_key, (N_SECTION, C, 1, 1), jnp.float32, math.log(0.3), math.log(3.0)))
    col_scale = jnp.exp(jax.random.uniform(third_key, (N_SECTION, 1, 1, C), jnp.float32, math.log(0.3), math.log(3.0)))
    return (base * row_scale * col_scale / math.sqrt(9.0 * C)).astype(jnp.bfloat16)


def plant(values, own_key, smallest, high):
    longest = values.shape.index(max(values.shape))
    spots = []
    for shift in (0, 1):
        where = [jax.random.randint(jax.random.fold_in(own_key, axis), (), 0, length) for axis, length in enumerate(values.shape)]
        where[longest] = (where[longest] + shift) % values.shape[longest]
        spots.append(tuple(where))
    return values.at[spots[0]].set(smallest).at[spots[1]].set(high)


def steps_of(rng, shape, cuts, smallest, high):
    def one(position, parts):
        steps = jax.random.uniform(jax.random.fold_in(jax.random.fold_in(rng, 6), position), (parts,), jnp.float32, smallest / len(cuts), high / len(cuts))
        return jnp.repeat(jnp.exp(steps), shape[position] // parts).reshape((-1,) + (1,) * (len(shape) - position - 1))

    factor_of = one(*cuts[0])
    for cut in cuts[1:]:
        factor_of = factor_of * one(*cut)
    return factor_of


def rank_table(amount, skew):
    weights = [(1 << 20) // math.isqrt(standing ** skew) + 1 for standing in range(1, amount + 1)]
    scale = 1 + sum(weights) // (1 << 30)
    return np.cumsum(np.array([max(1, weight // scale) for weight in weights]))


def skewed_ids(rng, extent, amount, skew):
    table = rank_table(amount, skew)
    ticket = jax.random.randint(jax.random.fold_in(rng, 1), extent, 0, int(table[amount - 1]))
    standing = jnp.searchsorted(jnp.asarray(table, jnp.int32), ticket, side="right")
    return jax.random.permutation(jax.random.fold_in(rng, 2), amount)[standing].astype(jnp.int32)


def centred(key, extent, deviation, limit, cuts=(), kind=jnp.bfloat16):
    array = deviation * jax.random.normal(key, extent, jnp.float32)
    if cuts:
        array = array * steps_of(key, extent, cuts, -0.22, 0.18)
    return jnp.clip(array, -limit, limit).astype(kind)


def setup_inputs(seed: int = 0) -> dict:
    streams_of = jax.random.split(jax.random.key(seed), 9)
    text_ids = plant(skewed_ids(streams_of[0], (BATCH, TXT_LEN), VOCAB, 2), jax.random.fold_in(streams_of[0], 3), 0, VOCAB - 1).astype(jnp.int32)
    seed_ids = plant(jax.random.randint(streams_of[1], (BATCH,), 0, SEEDS), jax.random.fold_in(streams_of[1], 1), 0, SEEDS - 1).astype(jnp.int32)
    text_table = centred(streams_of[2], (VOCAB, ZD), 4.0, 16.0, ((0, 8),))
    latent_table = centred(streams_of[3], (SEEDS, ZD), 1.0, 6.0, (), jnp.float32)
    start_map = centred(streams_of[4], (C, RES * RES), 1.0, 6.0)
    style_weight = centred(streams_of[5], (N_SECTION, C, ZD), ZD ** -0.5, 0.25, ((0, 4),))
    conv_weight = draw_conv_weight(jax.random.fold_in(streams_of[8], 71), 0)
    score_head = centred(streams_of[7], (C,), 1.0, 6.0, (), jnp.float32)
    return {"text_ids": text_ids, "seed_ids": seed_ids, "text_table": text_table, "latent_table": latent_table, "start_map": start_map, "style_weight": style_weight, "conv_weight": conv_weight, "score_head": score_head}


OFFSETS = tuple(((index_k // 3 - 1, index_k % 3 - 1) for index_k in range(9)))

def spread(feature, side_len):
    pixels = side_len * side_len
    column = lax.broadcasted_iota(jnp.int32, (1, pixels), 1) % side_len
    padded = jnp.pad(feature, ((0, 0), (side_len + 1, side_len + 1)))
    pieces = []
    for shift_down, shift_right in OFFSETS:
        offset = side_len + 1 + shift_down * side_len + shift_right
        inside = ((column + shift_right >= 0) & (column + shift_right < side_len)).astype(feature.dtype)
        pieces.append(lax.slice_in_dim(padded, offset, offset + pixels, axis=1) * inside)
    return jnp.concatenate(pieces, axis=0)

def spread_back(pieces, channels, side_len):
    pixels = side_len * side_len
    column = lax.broadcasted_iota(jnp.int32, (1, pixels), 1) % side_len
    result = jnp.zeros((channels, pixels), pieces.dtype)
    for index_k, (shift_down, shift_right) in enumerate(OFFSETS):
        inside = ((column + shift_right >= 0) & (column + shift_right < side_len)).astype(pieces.dtype)
        masked = pieces[index_k * channels:(index_k + 1) * channels] * inside
        padded = jnp.pad(masked, ((0, 0), (side_len + 1, side_len + 1)))
        begin_at = side_len + 1 - shift_down * side_len - shift_right
        result = result + lax.slice_in_dim(padded, begin_at, begin_at + pixels, axis=1)
    return result

def conv_one(flat_weight, sample):
    return jnp.dot(flat_weight, spread(sample, RES), preferred_element_type=jnp.float32)

def back_one(flat_weight, inputs):
    grad_piece, style_row = inputs
    back_prod = lax.dot_general(flat_weight, grad_piece, (((0,), (0,)), ((), ())), preferred_element_type=jnp.float32)
    return (style_row[:, None] * spread_back(back_prod, C, RES)).astype(jnp.bfloat16)

def add_term(running, inputs):
    grad_piece, mod_piece, factor_one = inputs
    term_now = lax.dot_general(grad_piece, spread(mod_piece, RES), (((1,), (1,)), ((), ())), preferred_element_type=jnp.float32)
    return (running + factor_one * term_now, None)

def reference(text_ids, seed_ids, text_table, latent_table, start_map, style_weight, conv_weight, score_head):
    pixels = RES * RES
    norm_div = pixels * math.sqrt(C)
    picked = jnp.take(text_table, text_ids, axis=0).astype(jnp.float32)
    text_mean = lax.optimization_barrier(jnp.sum(picked, axis=1)) / TXT_LEN
    gen_code = (jnp.take(latent_table, seed_ids, axis=0) + text_mean).astype(jnp.bfloat16)
    text_code = text_mean.astype(jnp.bfloat16)
    maps_now = jnp.broadcast_to(start_map, (BATCH, C, pixels))
    stored = []
    for layer_at in range(N_SECTION):
        code_now = gen_code if layer_at < GEN_SECTIONS else text_code
        styles = 1.0 + jnp.dot(code_now, style_weight[layer_at].T, preferred_element_type=jnp.float32)
        if layer_at < GEN_SECTIONS:
            squares = lax.optimization_barrier(jnp.sum(jnp.square(conv_weight[layer_at].astype(jnp.float32)), axis=1))
            demods = lax.rsqrt(jnp.dot(styles * styles, squares.T, precision=lax.Precision.HIGHEST) + 1e-08)
        else:
            demods = jnp.ones((BATCH, C), jnp.float32)
        flat_weight = conv_weight[layer_at].reshape(C, 9 * C)
        mod_input = (styles[:, :, None] * maps_now.astype(jnp.float32)).astype(jnp.bfloat16)
        conv_out = lax.map(partial(conv_one, flat_weight), mod_input)
        maps_now = jax.nn.silu(demods[:, :, None] * conv_out).astype(jnp.bfloat16)
        stored.append((styles, demods, mod_input, conv_out, flat_weight))
    scores = lax.optimization_barrier(jnp.sum(lax.optimization_barrier(jnp.sum(maps_now.astype(jnp.float32), axis=2)) * score_head, axis=1)) / norm_div
    d_factor = jax.nn.sigmoid(scores).astype(jnp.bfloat16)
    g_factor = (-jax.nn.sigmoid(-scores)).astype(jnp.bfloat16)
    unit_cot = (score_head / norm_div).astype(jnp.bfloat16)
    cotangent = jnp.broadcast_to(unit_cot[None, :, None], (BATCH, C, pixels))
    gradients = [None] * N_SECTION
    for layer_at in range(N_SECTION - 1, -1, -1):
        styles, demods, mod_input, conv_out, flat_weight = stored[layer_at]
        incoming = cotangent.astype(jnp.float32)
        if layer_at == GEN_SECTIONS - 1:
            incoming = incoming * g_factor.astype(jnp.float32)[:, None, None]
        pre_act = demods[:, :, None] * conv_out
        sigmas = jax.nn.sigmoid(pre_act)
        grad_pre = incoming * sigmas * (1.0 + pre_act * (1.0 - sigmas))
        grad_conv = (demods[:, :, None] * grad_pre).astype(jnp.bfloat16)
        if layer_at < GEN_SECTIONS:
            factors = jnp.ones((BATCH,), jnp.float32)
        else:
            factors = d_factor.astype(jnp.float32)
        weight_sum = lax.scan(add_term, jnp.zeros((C, 9 * C), jnp.float32), (grad_conv, mod_input, factors))[0]
        full_grad = weight_sum.reshape(C, 9, C)
        if layer_at < GEN_SECTIONS:
            grad_demod = lax.optimization_barrier(jnp.sum(grad_pre * conv_out, axis=2))
            demod_term = grad_demod * demods * demods * demods
            mixture = jnp.dot(demod_term.T, styles * styles, precision=lax.Precision.HIGHEST)
            full_grad = full_grad - conv_weight[layer_at].astype(jnp.float32) * mixture[:, None, :]
        gradients[layer_at] = full_grad
        if layer_at > 0:
            cotangent = lax.map(partial(back_one, flat_weight), (grad_conv, styles))
    return jnp.stack(gradients)
```

```python
import functools
import math

import jax
import jax.numpy as jnp
from jax import lax
from jax.experimental import pallas as pl
from jax.experimental.pallas import tpu as pltpu
from jax.sharding import PartitionSpec as P

TXT_LEN = 77
RES = 16
F32 = jnp.float32
BF16 = jnp.bfloat16
VMEM = pltpu.VMEM
LIMIT = 30 * 1024 * 1024


def params(limit=LIMIT):
    return pltpu.CompilerParams(vmem_limit_bytes=limit)


def swap(x, bit, count):
    return lax.ppermute(x, "dp", [(i, i ^ bit) for i in range(count)])


def column_masks(rows, side):
    column = lax.broadcasted_iota(jnp.int32, (rows, 1), 0) % side
    return column != 0, column != side - 1


def put_shifts(pieces, value, side, at, rows, pad):
    not_first, not_last = column_masks(rows, side)
    left = jnp.where(not_first, pltpu.roll(value, 1, 0), 0.0)
    right = jnp.where(not_last, pltpu.roll(value, rows - 1, 0), 0.0)
    for index, shifted in enumerate((left, value, right)):
        pieces[index, pl.ds(at, rows), :] = shifted.astype(BF16)


def blank_edges(pieces, rows, pad):
    blank = jnp.zeros((pad, pieces.shape[2]), BF16)
    for index in range(3):
        pieces[index, pl.ds(0, pad), :] = blank
        pieces[index, pl.ds(pad + rows, pad), :] = blank


def conv_of(pieces, spread, weight, sign, side, rows):
    channels = pieces.shape[2]
    for tap in range(9):
        down, across = sign * (tap // 3 - 1), sign * (tap % 3 - 1)
        spread[:, pl.ds(tap * channels, channels)] = pieces[
            across + 1, pl.ds(side + down * side, rows), :
        ]
    return jnp.dot(spread[...], weight[...], preferred_element_type=F32)


def forward_kernel(
    side, where, received, start, styles, demods, head, weight, kept_in, kept_conv,
    out, kept_in_out, kept_conv_out, score, pieces, spread, mod_box, conv_box, sems,
):
    rows = received.shape[0]
    position, slot, is_first = where[0], where[1], where[2]
    blank_edges(pieces, rows, side)
    style = styles[pl.ds(position, 1), :]
    source = jnp.where(is_first == 1, start[...].astype(F32), received[...].astype(F32))
    mod = (style * source).astype(BF16)
    mod_box[...] = mod
    first = pltpu.make_async_copy(mod_box, kept_in_out.at[slot], sems.at[0])
    first.start()
    put_shifts(pieces, mod.astype(F32), side, side, rows, side)
    conv = conv_of(pieces, spread, weight, 1, side, rows)
    conv_box[...] = conv
    second = pltpu.make_async_copy(conv_box, kept_conv_out.at[slot], sems.at[1])
    second.start()
    pre = demods[pl.ds(position, 1), :] * conv
    result = (pre / (1.0 + jnp.exp(-pre))).astype(BF16)
    out[...] = result
    sums = jnp.sum(result.astype(F32), axis=0, keepdims=True) * head[...]
    score[...] = jnp.broadcast_to(jnp.sum(sums, axis=1, keepdims=True), score.shape)
    first.wait()
    second.wait()


def backward_kernel(
    side, where, received, unit, styles, demods, scales, boosts, kept_conv, weight, kept_grad, kept_term,
    out, kept_grad_out, kept_term_out, pieces, spread, conv_box, grad_box, term_box, sems,
):
    rows = received.shape[0]
    position, slot, is_last = where[0], where[1], where[2]
    load = pltpu.make_async_copy(kept_conv.at[position], conv_box, sems.at[0])
    load.start()
    blank_edges(pieces, rows, side)
    demod = demods[pl.ds(position, 1), :]
    incoming = jnp.where(is_last == 1, jnp.broadcast_to(unit[...], received.shape), received[...].astype(F32))
    load.wait()
    conv = conv_box[...]
    pre = demod * conv
    sigma = 1.0 / (1.0 + jnp.exp(-pre))
    grad_pre = incoming * sigma * (1.0 + pre * (1.0 - sigma))
    grad_conv = demod * grad_pre
    grad_box[...] = (scales[pl.ds(position, 1), :] * grad_conv).astype(BF16)
    first = pltpu.make_async_copy(grad_box, kept_grad_out.at[slot], sems.at[1])
    first.start()
    term = jnp.sum(grad_pre * conv, axis=0, keepdims=True) * demod * demod * demod
    term_box[...] = jnp.broadcast_to(term, term_box.shape)
    second = pltpu.make_async_copy(term_box, kept_term_out.at[slot], sems.at[2])
    second.start()
    put_shifts(pieces, grad_conv.astype(BF16).astype(F32), side, side, rows, side)
    back = conv_of(pieces, spread, weight, -1, side, rows)
    out[...] = (styles[pl.ds(position, 1), :] * boosts[pl.ds(position, 1), :] * back).astype(BF16)
    first.wait()
    second.wait()


def weight_grad_kernel(
    side, micro, count, orders, taps, where, kept_grad, kept_in, squares, terms, weight, *rest
):
    outs, (pieces, grad_rows, by_out, mixture, mod_f) = rest[:-5], rest[-5:]
    channels = kept_in.shape[2]
    pixels = kept_in.shape[1]
    part = channels // count
    band = micro * side
    here = where[0]
    blank = jnp.zeros((band, channels), BF16)
    for index in range(3):
        pieces[index, pl.ds(0, band), :] = blank
        pieces[index, pl.ds(band + micro * pixels, band), :] = blank
    for sample in range(micro):
        for line in range(side):
            at = line * band + sample * side
            grad_rows[pl.ds(at, side), :] = kept_grad[sample, pl.ds(line * side, side), :]
            mod_f[pl.ds(at, side), :] = kept_in[sample, pl.ds(line * side, side), :]
    put_shifts(pieces, mod_f[...].astype(F32), side, band, micro * pixels, band)
    turned = jnp.transpose(grad_rows[...].astype(F32)).astype(BF16)
    mixture[...] = lax.dot_general(
        terms[...], squares[...], (((0,), (0,)), ((), ())),
        preferred_element_type=F32, precision=lax.Precision.HIGHEST,
    )
    by_out[len(orders)] = turned
    for kind, order in enumerate(orders):
        for slot in range(count):
            flip = 0
            for stage, bit in enumerate(order):
                flip |= ((slot >> (len(order) - 1 - stage)) & 1) << bit
            source = pl.multiple_of((here ^ flip) * part, part)
            by_out[kind, pl.ds(slot * part, part), :] = by_out[len(orders), pl.ds(source, part), :]
    for chunk, (kind, tap_list) in enumerate(taps):
        keep, send = outs[2 * chunk], outs[2 * chunk + 1]
        order = orders[kind]
        for spot, tap in enumerate(tap_list):
            total = jnp.dot(
                by_out[kind], pieces[tap % 3, pl.ds((tap // 3) * band, micro * pixels), :],
                preferred_element_type=F32,
            )
            for slot in range(count):
                flip = 0
                for stage, bit in enumerate(order):
                    flip |= ((slot >> (len(order) - 1 - stage)) & 1) << bit
                source = pl.multiple_of((here ^ flip) * part, part)
                fixed = total[slot * part : (slot + 1) * part] - weight[
                    tap, pl.ds(source, part), :
                ].astype(F32) * mixture[pl.ds(source, part), :]
                target = keep if slot < count // 2 else send
                target[slot % (count // 2), spot] = fixed.astype(BF16)


def on_device(
    text_ids, seed_ids, text_table, latent_table, start_map, style_weight, conv_weight, score_head
):
    sections = lax.axis_size("section")
    count = lax.axis_size("dp")
    bits = count.bit_length() - 1
    gen_count = sections - sections // 4
    section_at = lax.axis_index("section")
    here = lax.axis_index("dp")
    is_gen = section_at < gen_count
    micro = seed_ids.shape[0]
    channels, pixels = start_map.shape
    side = RES
    vocab_rows = text_table.shape[0]
    norm_div = pixels * math.sqrt(channels)

    ids = text_ids[None]
    for stage in range(bits):
        ids = jnp.concatenate([ids, swap(ids, 1 << stage, count)], axis=0)
    wanted = ids.reshape(count * micro, TXT_LEN) - here * vocab_rows
    rows = lax.broadcasted_iota(jnp.int32, (1, 1, vocab_rows), 2)
    hits = jnp.sum((wanted[:, :, None] == rows).astype(F32), axis=1)
    sums = jnp.dot(hits.astype(BF16), text_table, preferred_element_type=F32)
    sums = sums.reshape(count, micro, channels)
    for stage in reversed(range(bits)):
        half = 1 << stage
        sums = sums[:half] + swap(sums[half:], half, count)
    text_mean = sums[0] / TXT_LEN

    weight = conv_weight[0]
    weight_out = jnp.transpose(weight, (1, 0, 2))
    weight_in = jnp.transpose(weight, (1, 2, 0)).reshape(9 * channels, channels)
    squares = jnp.sum(jnp.square(weight_out.astype(F32)), axis=0)

    latent = jnp.take(latent_table, seed_ids, axis=0) + text_mean
    code_now = jnp.where(is_gen, latent, text_mean).astype(BF16)
    styles = 1.0 + lax.dot_general(
        code_now, style_weight[0], (((1,), (1,)), ((), ())), preferred_element_type=F32
    )
    demods = lax.rsqrt(
        lax.dot_general(
            styles * styles, squares, (((1,), (1,)), ((), ())), precision=lax.Precision.HIGHEST
        )
        + 1e-08
    )
    demods = jnp.where(is_gen, demods, jnp.ones_like(demods))
    first_map = start_map.T
    head = score_head[None]
    ticks = micro + sections - 1

    whole = pl.BlockSpec(memory_space=VMEM)
    anywhere = pl.BlockSpec(memory_space=pl.ANY)
    smem = pl.BlockSpec(memory_space=pltpu.SMEM)
    flops = 2 * 9 * channels * channels * pixels
    conv_cost = pl.CostEstimate(
        flops=flops, bytes_accessed=9 * channels * channels * 2 + 5 * channels * pixels * 2,
        transcendentals=channels * pixels,
    )
    tall = 2 * side + pixels
    conv_scratch = [VMEM((3, tall, channels), BF16), VMEM((pixels, 9 * channels), BF16)]
    forward = pl.pallas_call(
        functools.partial(forward_kernel, side),
        in_specs=[smem] + [whole] * 6 + [anywhere] * 2,
        out_specs=[whole, anywhere, anywhere, whole],
        out_shape=[
            jax.ShapeDtypeStruct((pixels, channels), BF16),
            jax.ShapeDtypeStruct((micro + 1, pixels, channels), BF16),
            jax.ShapeDtypeStruct((micro + 1, pixels, channels), F32),
            jax.ShapeDtypeStruct((8, 128), F32),
        ],
        scratch_shapes=conv_scratch
        + [
            VMEM((pixels, channels), BF16),
            VMEM((pixels, channels), F32),
            pltpu.SemaphoreType.DMA((2,)),
        ],
        input_output_aliases={7: 1, 8: 2},
        cost_estimate=conv_cost,
        compiler_params=params(),
        name="forward_conv",
    )
    backward = pl.pallas_call(
        functools.partial(backward_kernel, side),
        in_specs=[smem] + [whole] * 6 + [anywhere, whole, anywhere, anywhere],
        out_specs=[whole, anywhere, anywhere],
        out_shape=[
            jax.ShapeDtypeStruct((pixels, channels), BF16),
            jax.ShapeDtypeStruct((micro + 1, pixels, channels), BF16),
            jax.ShapeDtypeStruct((micro + 1, 8, channels), F32),
        ],
        scratch_shapes=conv_scratch
        + [
            VMEM((pixels, channels), F32),
            VMEM((pixels, channels), BF16),
            VMEM((8, channels), F32),
            pltpu.SemaphoreType.DMA((3,)),
        ],
        input_output_aliases={9: 1, 10: 2},
        cost_estimate=conv_cost,
        compiler_params=params(),
        name="backward_conv",
    )

    kept_in = jnp.zeros((micro + 1, pixels, channels), BF16)
    kept_conv = jnp.zeros((micro + 1, pixels, channels), F32)
    outgoing = first_map
    scores = []
    for tick in range(ticks):
        received = (
            lax.ppermute(outgoing, "section", [(i, i + 1) for i in range(sections - 1) if 0 <= tick - 1 - i < micro])
            if tick
            else first_map
        )
        position = tick - section_at
        active = (position >= 0) & (position < micro)
        position = jnp.clip(position, 0, micro - 1)
        where = jnp.stack(
            [position, jnp.where(active, position, micro), (section_at == 0).astype(jnp.int32)]
        ).astype(jnp.int32)
        outgoing, kept_in, kept_conv, score = forward(
            where, received, first_map, styles, demods, head, weight_in, kept_in, kept_conv
        )
        scores.append(score[0, 0])
    scores = jnp.stack(scores[sections - 1 :])[:, None] / norm_div
    for hop in range(sections - gen_count - 1):
        target = sections - 2 - hop
        passed = lax.ppermute(scores, "section", [(target + 1, target)])
        scores = jnp.where(section_at == target, passed, scores)
    d_factor = jax.nn.sigmoid(scores).astype(BF16).astype(F32)
    g_factor = (-jax.nn.sigmoid(-scores)).astype(BF16).astype(F32)
    ones = jnp.ones((micro, channels), F32)
    scales = jnp.where(is_gen, ones, d_factor * ones)
    boosts = jnp.where(section_at == gen_count, g_factor * ones, ones)
    unit = (head / norm_div).astype(BF16).astype(F32)

    kept_grad = jnp.zeros((micro + 1, pixels, channels), BF16)
    kept_term = jnp.zeros((micro + 1, 8, channels), F32)
    outgoing = None
    for tick in range(ticks):
        received = (
            lax.ppermute(
                outgoing, "section",
                [(i, i - 1) for i in range(1, sections) if 0 <= tick - 1 - (sections - 1 - i) < micro],
            )
            if tick
            else first_map
        )
        position = tick - (sections - 1 - section_at)
        active = (position >= 0) & (position < micro)
        position = jnp.clip(position, 0, micro - 1)
        where = jnp.stack(
            [position, jnp.where(active, position, micro), (section_at == sections - 1).astype(jnp.int32)]
        ).astype(jnp.int32)
        outgoing, kept_grad, kept_term = backward(
            where, received, unit, styles, demods, scales, boosts, kept_conv,
            weight_out.reshape(9 * channels, channels), kept_grad, kept_term,
        )

    terms = jnp.where(is_gen, kept_term[:micro, 0, :], 0.0)
    pad = (-micro) % 8
    terms = jnp.pad(terms, ((0, pad), (0, 0)))
    style_squares = jnp.pad(styles * styles, ((0, pad), (0, 0)))
    part = channels // count
    orders = (tuple(range(bits)), (1, 0) + tuple(range(2, bits)))
    taps = ((0, (0, 1, 2)), (0, (3, 4)), (1, (7, 8)), (0, (5, 6)))
    shapes = []
    for kind, tap_list in taps:
        shapes += [jax.ShapeDtypeStruct((count // 2, len(tap_list), part, channels), BF16)] * 2
    tall = micro * (2 * side + pixels)
    pairs = pl.pallas_call(
        functools.partial(weight_grad_kernel, side, micro, count, orders, taps),
        in_specs=[smem] + [whole] * 5,
        out_specs=[whole] * len(shapes),
        out_shape=shapes,
        scratch_shapes=[
            VMEM((3, tall, channels), BF16),
            VMEM((micro * pixels, channels), BF16),
            VMEM((len(orders) + 1, channels, micro * pixels), BF16),
            VMEM((channels, channels), F32),
            VMEM((micro * pixels, channels), BF16),
        ],
        cost_estimate=pl.CostEstimate(flops=micro * flops, bytes_accessed=20 * 1024 * 1024, transcendentals=0),
        compiler_params=params(48 * 1024 * 1024),
        name="weight_grad",
    )(here[None].astype(jnp.int32), kept_grad, kept_in, style_squares, terms, weight_out)
    done = [None] * 9
    for chunk, (kind, tap_list) in enumerate(taps):
        keep, send = pairs[2 * chunk], pairs[2 * chunk + 1]
        for stage in range(bits):
            got = swap(send, 1 << orders[kind][stage], count)
            total = keep.astype(F32) + got.astype(F32)
            half = total.shape[0] // 2
            if half:
                keep = total[:half]
                send = total[half:].astype(BF16)
        for spot, tap in enumerate(tap_list):
            done[tap] = total[0, spot]
    return jnp.stack(done, axis=1)[None]


def solution(mesh):
    placed = (
        P("dp", None),
        P("dp"),
        P("dp", None),
        P(),
        P(),
        P("section", None, None),
        P("section", None, None, None),
        P(),
    )
    return jax.shard_map(
        on_device,
        mesh=mesh,
        in_specs=placed,
        out_specs=P("section", "dp", None, None),
        check_vma=False,
    )
```

```python
import functools
import math

import jax
import jax.numpy as jnp
from jax import lax
from jax.experimental import pallas as pl
from jax.experimental.pallas import tpu as pltpu
from jax.sharding import PartitionSpec as P

TXT_LEN = 77
RES = 16
F32 = jnp.float32
BF16 = jnp.bfloat16
VMEM = pltpu.VMEM
LIMIT = 48 * 1024 * 1024
SLOTS = 24


def params():
    return pltpu.CompilerParams(vmem_limit_bytes=LIMIT)


def swap(x, bit, count):
    return lax.ppermute(x, "dp", [(i, i ^ bit) for i in range(count)])


def column_masks(rows, side):
    column = lax.broadcasted_iota(jnp.int32, (rows, 1), 0) % side
    return column != 0, column != side - 1


def put_shifts(pieces, value, side, at, rows, pad):
    not_first, not_last = column_masks(rows, side)
    left = jnp.where(not_first, pltpu.roll(value, 1, 0), 0.0)
    right = jnp.where(not_last, pltpu.roll(value, rows - 1, 0), 0.0)
    for index, shifted in enumerate((left, value, right)):
        pieces[index, pl.ds(at, rows), :] = shifted.astype(BF16)


def blank_edges(pieces, rows, pad):
    blank = jnp.zeros((pad, pieces.shape[2]), BF16)
    for index in range(3):
        pieces[index, pl.ds(0, pad), :] = blank
        pieces[index, pl.ds(pad + rows, pad), :] = blank


def conv_of(pieces, weight, sign, side, rows):
    channels = pieces.shape[2]
    total = None
    for tap in range(9):
        down, across = sign * (tap // 3 - 1), sign * (tap % 3 - 1)
        term = jnp.dot(
            pieces[across + 1, pl.ds(side + down * side, rows), :],
            weight[pl.ds(tap * channels, channels), :],
            preferred_element_type=F32,
        )
        total = term if total is None else total + term
    return total


def forward_kernel(tick, side, micro, *refs):
    if tick:
        received, start, pack, head, weight = refs[:5]
        refs = refs[7:]
    else:
        start, pack, head, weight = refs[:4]
        received = start
        refs = refs[4:]
    out, kept_in, kept_conv, score, pieces, mod_box, conv_box, sems = refs
    rows = start.shape[0]
    section = lax.axis_index("section")
    position = tick - section

    @pl.when((position >= 0) & (position < micro))
    def _():
        blank_edges(pieces, rows, side)
        style = pack[pl.ds(position, 1), :]
        source = received[...]
        if tick:
            source = jnp.where(section == 0, start[...].astype(F32), source.astype(F32))
        mod = (style * source.astype(F32)).astype(BF16)
        mod_box[...] = mod.reshape(mod_box.shape)
        first = pltpu.make_async_copy(mod_box, kept_in.at[:, position], sems.at[0])
        first.start()
        put_shifts(pieces, mod.astype(F32), side, side, rows, side)
        conv = conv_of(pieces, weight, 1, side, rows)
        conv_box[...] = conv
        second = pltpu.make_async_copy(conv_box, kept_conv.at[position], sems.at[1])
        second.start()
        pre = pack[pl.ds(8 + position, 1), :] * conv
        result = (pre / (1.0 + jnp.exp(-pre))).astype(BF16)
        out[...] = result
        sums = jnp.sum(result.astype(F32), axis=0, keepdims=True) * head[...]
        score[...] = jnp.broadcast_to(jnp.sum(sums, axis=1, keepdims=True), score.shape)
        first.wait()
        second.wait()


def backward_kernel(tick, side, micro, norm_div, *refs):
    if tick:
        received = refs[0]
        refs = refs[1:]
    head, pack = refs[:2]
    scores, refs = refs[2 : 2 + micro], refs[2 + micro :]
    kept_conv, weight = refs[:2]
    refs = refs[4:] if tick else refs[2:]
    out, kept_grad, kept_term, pieces, conv_box, grad_box, term_box, sems = refs
    rows = conv_box.shape[0]
    section = lax.axis_index("section")
    sections = lax.axis_size("section")
    gen_count = sections - sections // 4
    position = tick - (sections - 1 - section)

    @pl.when((position >= 0) & (position < micro))
    def _():
        load = pltpu.make_async_copy(kept_conv.at[position], conv_box, sems.at[0])
        load.start()
        blank_edges(pieces, rows, side)
        raw = scores[0][...]
        for index in range(1, micro):
            raw = jnp.where(position == index, scores[index][...], raw)
        raw = raw[:1, :1] / norm_div
        d_factor = (1.0 / (1.0 + jnp.exp(-raw))).astype(BF16).astype(F32)
        g_factor = (-1.0 / (1.0 + jnp.exp(raw))).astype(BF16).astype(F32)
        scale = jnp.where(section < gen_count, jnp.ones_like(raw), d_factor)
        boost = jnp.where(section == gen_count, g_factor, jnp.ones_like(raw))
        demod = pack[pl.ds(8 + position, 1), :]
        unit = (head[...] / norm_div).astype(BF16).astype(F32)
        incoming = jnp.broadcast_to(unit, conv_box.shape)
        if tick:
            incoming = jnp.where(section == sections - 1, incoming, received[...].astype(F32))
        load.wait()
        conv = conv_box[...]
        pre = demod * conv
        sigma = 1.0 / (1.0 + jnp.exp(-pre))
        grad_pre = incoming * sigma * (1.0 + pre * (1.0 - sigma))
        grad_conv = demod * grad_pre
        grad_box[...] = (scale * grad_conv).astype(BF16).reshape(grad_box.shape)
        first = pltpu.make_async_copy(grad_box, kept_grad.at[:, position], sems.at[1])
        first.start()
        term = jnp.sum(grad_pre * conv, axis=0, keepdims=True) * demod * demod * demod
        term = jnp.where(section < gen_count, term, 0.0)
        term_box[...] = jnp.broadcast_to(term, term_box.shape)
        second = pltpu.make_async_copy(term_box, kept_term.at[position], sems.at[2])
        second.start()
        put_shifts(pieces, grad_conv.astype(BF16).astype(F32), side, side, rows, side)
        back = conv_of(pieces, weight, -1, side, rows)
        out[...] = (pack[pl.ds(position, 1), :] * boost * back).astype(BF16)
        first.wait()
        second.wait()


def slot_flip(slot, order):
    flip = 0
    for stage, bit in enumerate(order):
        flip |= ((slot >> (len(order) - 1 - stage)) & 1) << bit
    return flip


def weight_grad_kernel(
    side, micro, count, orders, taps, kept_grad, kept_in, kept_term, pack, weight, *rest
):
    outs, rest = rest[: 2 * len(taps)], rest[2 * len(taps) :]
    pieces, grad_rows, mod_rows, terms, by_out, mixture, sems = rest
    channels = kept_in.shape[3]
    total_rows = micro * side * side
    part = channels // count
    band = micro * side
    here = lax.axis_index("dp")
    chosen = pl.ds(0, micro)
    loads = [
        pltpu.make_async_copy(kept_grad.at[:, chosen], grad_rows, sems.at[0]),
        pltpu.make_async_copy(kept_in.at[:, chosen], mod_rows, sems.at[1]),
        pltpu.make_async_copy(kept_term.at[chosen], terms, sems.at[2]),
    ]
    for load in loads:
        load.start()
    blank = jnp.zeros((band, channels), BF16)
    for index in range(3):
        pieces[index, pl.ds(0, band), :] = blank
        pieces[index, pl.ds(band + total_rows, band), :] = blank
    loads[1].wait()
    put_shifts(
        pieces, mod_rows[...].reshape(total_rows, channels).astype(F32), side, band, total_rows, band
    )
    loads[0].wait()
    turned = jnp.transpose(grad_rows[...].reshape(total_rows, channels).astype(F32)).astype(BF16)
    by_out[len(orders)] = turned
    loads[2].wait()
    row = lax.broadcasted_iota(jnp.int32, (8, channels), 0)
    stacked = jnp.zeros((8, channels), F32)
    for sample in range(micro):
        stacked = jnp.where(row == sample, terms[sample], stacked)
    mixture[...] = lax.dot_general(
        stacked, pack[pl.ds(0, 8), :] * pack[pl.ds(0, 8), :], (((0,), (0,)), ((), ())),
        preferred_element_type=F32, precision=lax.Precision.HIGHEST,
    )
    for kind, order in enumerate(orders):
        for slot in range(count):
            source = pl.multiple_of((here ^ slot_flip(slot, order)) * part, part)
            by_out[kind, pl.ds(slot * part, part), :] = by_out[len(orders), pl.ds(source, part), :]
    for chunk, (kind, tap_list) in enumerate(taps):
        keep, send = outs[2 * chunk], outs[2 * chunk + 1]
        for spot, tap in enumerate(tap_list):
            total = jnp.dot(
                by_out[kind], pieces[tap % 3, pl.ds((tap // 3) * band, total_rows), :],
                preferred_element_type=F32,
            )
            for slot in range(count):
                source = pl.multiple_of((here ^ slot_flip(slot, orders[kind])) * part, part)
                fixed = total[slot * part : (slot + 1) * part] - weight[
                    pl.ds(tap * channels + source, part), :
                ].astype(F32) * mixture[pl.ds(source, part), :]
                target = keep if slot < count // 2 else send
                target[slot % (count // 2), spot] = fixed.astype(BF16)


def on_device(
    text_ids, seed_ids, text_table, latent_table, start_map, style_weight, conv_weight, score_head
):
    sections = lax.axis_size("section")
    count = lax.axis_size("dp")
    bits = count.bit_length() - 1
    gen_count = sections - sections // 4
    section_at = lax.axis_index("section")
    here = lax.axis_index("dp")
    is_gen = section_at < gen_count
    micro = seed_ids.shape[0]
    channels, pixels = start_map.shape
    side = RES
    vocab_rows = text_table.shape[0]
    norm_div = pixels * math.sqrt(channels)

    ids = text_ids[None]
    weight = conv_weight[0]
    weight_out = jnp.transpose(weight, (1, 0, 2))
    weight_in = jnp.transpose(weight, (1, 2, 0)).reshape(9 * channels, channels)
    first_map = start_map.T
    latent = jnp.take(latent_table, seed_ids, axis=0)
    for stage in range(bits):
        other = swap(ids, 1 << stage, count)
        if stage == 0:
            other, weight_in, first_map, latent = lax.optimization_barrier(
                (other, weight_in, first_map, latent)
            )
        ids = jnp.concatenate([ids, other], axis=0)
    wanted = ids.reshape(count * micro, TXT_LEN) - here * vocab_rows
    rows = lax.broadcasted_iota(jnp.int32, (1, 1, vocab_rows), 2)
    hits = jnp.sum((wanted[:, :, None] == rows).astype(F32), axis=1)
    sums = jnp.dot(hits.astype(BF16), text_table, preferred_element_type=F32)
    sums = sums.reshape(count, micro, channels)
    for stage in reversed(range(bits)):
        half = 1 << stage
        sums = sums[:half] + swap(sums[half:], half, count)
    text_mean = sums[0] / TXT_LEN

    squares = jnp.sum(jnp.square(weight_out.astype(F32)), axis=0)

    code_now = jnp.where(is_gen, latent + text_mean, text_mean).astype(BF16)
    styles = 1.0 + lax.dot_general(
        code_now, style_weight[0], (((1,), (1,)), ((), ())), preferred_element_type=F32
    )
    demods = lax.rsqrt(
        lax.dot_general(
            styles * styles, squares, (((1,), (1,)), ((), ())), precision=lax.Precision.HIGHEST
        )
        + 1e-08
    )
    demods = jnp.where(is_gen, demods, jnp.ones_like(demods))
    rest = ((0, 8 - micro), (0, 0))
    pack = jnp.concatenate([jnp.pad(styles, rest), jnp.pad(demods, rest)], axis=0)
    head = score_head[None]
    ticks = micro + sections - 1

    whole = pl.BlockSpec(memory_space=VMEM)
    far = pl.BlockSpec(memory_space=pltpu.HBM)
    flops = 2 * 9 * channels * channels * pixels
    conv_cost = pl.CostEstimate(
        flops=flops, bytes_accessed=9 * channels * channels * 2 + 5 * channels * pixels * 2,
        transcendentals=channels * pixels,
    )
    tall = 2 * side + pixels
    conv_scratch = [VMEM((3, tall, channels), BF16)]
    plain = jax.ShapeDtypeStruct((pixels, channels), BF16)
    lined = jax.ShapeDtypeStruct((side, SLOTS, side, channels), BF16)
    tower = jax.ShapeDtypeStruct((SLOTS, pixels, channels), F32)
    rows_kept = jax.ShapeDtypeStruct((1024, 8, channels), F32)

    def forward(tick, arrays):
        return pl.pallas_call(
            functools.partial(forward_kernel, tick, side, micro),
            in_specs=[whole] * 5 + [far] * 2 if tick else [whole] * 4,
            out_specs=[whole, far, far, whole],
            out_shape=[plain, lined, tower, jax.ShapeDtypeStruct((8, 128), F32)],
            scratch_shapes=conv_scratch
            + [
                VMEM((side, side, channels), BF16),
                VMEM((pixels, channels), F32),
                pltpu.SemaphoreType.DMA((2,)),
            ],
            input_output_aliases={5: 1, 6: 2} if tick else {},
            cost_estimate=conv_cost,
            compiler_params=params(),
            name="forward_conv",
        )(*arrays)

    def backward(tick, arrays):
        fixed = 3 + micro if tick else 2 + micro
        return pl.pallas_call(
            functools.partial(backward_kernel, tick, side, micro, norm_div),
            in_specs=[whole] * fixed + [far, whole] + [far] * (2 if tick else 0),
            out_specs=[whole, far, far],
            out_shape=[plain, lined, rows_kept],
            scratch_shapes=conv_scratch
            + [
                VMEM((pixels, channels), F32),
                VMEM((side, side, channels), BF16),
                VMEM((8, channels), F32),
                pltpu.SemaphoreType.DMA((3,)),
            ],
            input_output_aliases={fixed + 2: 1, fixed + 3: 2} if tick else {},
            cost_estimate=conv_cost,
            compiler_params=params(),
            name="backward_conv",
        )(*arrays)

    scores = []
    kept_in = kept_conv = outgoing = None
    for tick in range(ticks):
        if tick:
            received = lax.ppermute(
                outgoing, "section", [(i, i + 1) for i in range(sections - 1) if 0 <= tick - 1 - i < micro]
            )
            arrays = (received, first_map, pack, head, weight_in, kept_in, kept_conv)
        else:
            arrays = (first_map, pack, head, weight_in)
        outgoing, kept_in, kept_conv, score = forward(tick, arrays)
        scores.append(score)
    scores = scores[sections - 1 :]
    for hop in range(sections - gen_count - 1):
        target = sections - 2 - hop
        passed = lax.ppermute(scores, "section", [(target + 1, target)])
        scores = [jnp.where(section_at == target, new, old) for new, old in zip(passed, scores)]

    flat_out = weight_out.reshape(9 * channels, channels)
    kept_grad = kept_term = outgoing = None
    for tick in range(ticks):
        arrays = (head, pack, *scores, kept_conv, flat_out)
        if tick:
            received = lax.ppermute(
                outgoing, "section",
                [(i, i - 1) for i in range(1, sections) if 0 <= tick - 1 - (sections - 1 - i) < micro],
            )
            arrays = (received, *arrays, kept_grad, kept_term)
        outgoing, kept_grad, kept_term = backward(tick, arrays)

    part = channels // count
    orders = (tuple(range(bits)), (1, 0) + tuple(range(2, bits)))
    taps = ((0, (0, 1, 2)), (0, (3, 4)), (1, (7, 8)), (0, (5, 6)))
    shapes = []
    for kind, tap_list in taps:
        shapes += [jax.ShapeDtypeStruct((count // 2, len(tap_list), part, channels), BF16)] * 2
    pairs = pl.pallas_call(
        functools.partial(weight_grad_kernel, side, micro, count, orders, taps),
        in_specs=[far] * 3 + [whole] * 2,
        out_specs=[whole] * len(shapes),
        out_shape=shapes,
        scratch_shapes=[
            VMEM((3, micro * tall, channels), BF16),
            VMEM((side, micro, side, channels), BF16),
            VMEM((side, micro, side, channels), BF16),
            VMEM((micro, 8, channels), F32),
            VMEM((len(orders) + 1, channels, micro * pixels), BF16),
            VMEM((channels, channels), F32),
            pltpu.SemaphoreType.DMA((3,)),
        ],
        cost_estimate=pl.CostEstimate(flops=micro * flops, bytes_accessed=20 * 1024 * 1024, transcendentals=0),
        compiler_params=params(),
        name="weight_grad",
    )(kept_grad, kept_in, kept_term, pack, flat_out)
    done = [None] * 9
    for chunk, (kind, tap_list) in enumerate(taps):
        keep, send = pairs[2 * chunk], pairs[2 * chunk + 1]
        for stage in range(bits):
            got = swap(send, 1 << orders[kind][stage], count)
            total = keep.astype(F32) + got.astype(F32)
            half = total.shape[0] // 2
            if half:
                keep = total[:half]
                send = total[half:].astype(BF16)
        for spot, tap in enumerate(tap_list):
            done[tap] = total[0, spot]
    return jnp.stack(done, axis=1)[None]


def solution(mesh):
    placed = (
        P("dp", None),
        P("dp"),
        P("dp", None),
        P(),
        P(),
        P("section", None, None),
        P("section", None, None, None),
        P(),
    )
    return jax.shard_map(
        on_device,
        mesh=mesh,
        in_specs=placed,
        out_specs=P("section", "dp", None, None),
        check_vma=False,
    )
```

```python
import functools
import math

import jax
import jax.numpy as jnp
from jax import lax
from jax.experimental import pallas as pl
from jax.experimental.pallas import tpu as pltpu
from jax.sharding import PartitionSpec as P


TXT_LEN = 77
RES = 16
F32 = jnp.float32
BF16 = jnp.bfloat16
VMEM = pltpu.VMEM
LIMIT = 40 * 1024 * 1024
SLOTS = 60


def params():
    return pltpu.CompilerParams(vmem_limit_bytes=LIMIT)


def swap(x, bit, count):
    return lax.ppermute(x, "dp", [(i, i ^ bit) for i in range(count)])


def column_masks(rows, side):
    column = lax.broadcasted_iota(jnp.int32, (rows, 1), 0) % side
    return column != 0, column != side - 1


def put_shifts(pieces, value, side, at, rows):
    not_first, not_last = column_masks(rows, side)
    left = jnp.where(not_first, pltpu.roll(value, 1, 0), 0.0)
    right = jnp.where(not_last, pltpu.roll(value, rows - 1, 0), 0.0)
    for index, shifted in enumerate((left, value, right)):
        pieces[index, pl.ds(at, rows), :] = shifted.astype(BF16)


def blank_edges(pieces, rows, pad):
    blank = jnp.zeros((pad, pieces.shape[2]), BF16)
    for index in range(3):
        pieces[index, pl.ds(0, pad), :] = blank
        pieces[index, pl.ds(pad + rows, pad), :] = blank


def conv_of(pieces, weight, sign, side, rows):
    channels = pieces.shape[2]
    total = None
    for tap in range(9):
        down, across = sign * (tap // 3 - 1), sign * (tap % 3 - 1)
        term = lax.dot_general(
            pieces[across + 1, pl.ds(side + down * side, rows), :],
            weight[pl.ds(tap * channels, channels), :],
            (((1,), ((1 if sign > 0 else 0),)), ((), ())),
            preferred_element_type=F32,
        )
        total = term if total is None else total + term
    return total


def forward_kernel(tick, side, micro, *refs):
    if tick:
        received, start, pack, head, weight = refs[:5]
        refs = refs[7:]
    else:
        start, pack, head, weight = refs[:4]
        received = start
        refs = refs[4:]
    out, kept_in, kept_conv, score, pieces, mod_box, conv_box, sems = refs
    rows = start.shape[0]
    section = lax.axis_index("section")
    position = tick - section

    @pl.when((position >= 0) & (position < micro))
    def _():
        blank_edges(pieces, rows, side)
        style = pack[pl.ds(position, 1), :]
        source = received[...]
        if tick:
            source = jnp.where(section == 0, start[...].astype(F32), source.astype(F32))
        mod = (style * source.astype(F32)).astype(BF16)
        mod_box[pl.ds(0, side)] = mod.reshape(side, side, mod.shape[1])
        squared = style * style
        high = squared.astype(BF16).astype(F32)
        row = lax.broadcasted_iota(jnp.int32, (side, mod.shape[1]), 0)
        mod_box[side] = jnp.where(row == 0, high, jnp.where(row == 1, squared - high, 0.0)).astype(BF16)
        first = pltpu.make_async_copy(mod_box, kept_in.at[:, position], sems.at[0])
        first.start()
        put_shifts(pieces, mod.astype(F32), side, side, rows)
        conv = conv_of(pieces, weight, 1, side, rows)
        conv_box[...] = conv
        second = pltpu.make_async_copy(conv_box, kept_conv.at[position], sems.at[1])
        second.start()
        pre = pack[pl.ds(8 + position, 1), :] * conv
        result = (pre / (1.0 + jnp.exp(-pre))).astype(BF16)
        out[...] = result
        sums = jnp.sum(result.astype(F32), axis=0, keepdims=True) * head[...]
        score[...] = jnp.broadcast_to(jnp.sum(sums, axis=1, keepdims=True), score.shape)
        first.wait()
        second.wait()


def backward_kernel(tick, side, micro, norm_div, *refs):
    if tick:
        received = refs[0]
        refs = refs[1:]
    head, pack = refs[:2]
    scores, refs = refs[2 : 2 + micro], refs[2 + micro :]
    kept_conv, weight = refs[:2]
    refs = refs[3:] if tick else refs[2:]
    out, kept_grad, pieces, conv_box, grad_box, sems = refs
    rows = conv_box.shape[0]
    section = lax.axis_index("section")
    sections = lax.axis_size("section")
    gen_count = sections - sections // 4
    position = tick - (sections - 1 - section)

    @pl.when((position >= 0) & (position < micro))
    def _():
        load = pltpu.make_async_copy(kept_conv.at[position], conv_box, sems.at[0])
        load.start()
        blank_edges(pieces, rows, side)
        raw = scores[0][...]
        for index in range(1, micro):
            raw = jnp.where(position == index, scores[index][...], raw)
        raw = raw[:1, :1] / norm_div
        d_factor = (1.0 / (1.0 + jnp.exp(-raw))).astype(BF16).astype(F32)
        g_factor = (-1.0 / (1.0 + jnp.exp(raw))).astype(BF16).astype(F32)
        scale = jnp.where(section < gen_count, jnp.ones_like(raw), d_factor)
        boost = jnp.where(section == gen_count, g_factor, jnp.ones_like(raw))
        demod = pack[pl.ds(8 + position, 1), :]
        unit = (head[...] / norm_div).astype(BF16).astype(F32)
        incoming = jnp.broadcast_to(unit, conv_box.shape)
        if tick:
            incoming = jnp.where(section == sections - 1, incoming, received[...].astype(F32))
        load.wait()
        conv = conv_box[...]
        pre = demod * conv
        sigma = 1.0 / (1.0 + jnp.exp(-pre))
        grad_pre = incoming * sigma * (1.0 + pre * (1.0 - sigma))
        grad_conv = demod * grad_pre
        channels = conv.shape[1]
        grad_box[pl.ds(0, side)] = (scale * grad_conv).astype(BF16).reshape(side, side, channels)
        term = jnp.sum(grad_pre * conv, axis=0, keepdims=True) * demod * demod * demod
        term = jnp.where(section < gen_count, term, 0.0)
        high = term.astype(BF16).astype(F32)
        row = lax.broadcasted_iota(jnp.int32, (side, channels), 0)
        grad_box[side] = jnp.where(row == 0, high, jnp.where(row == 1, term - high, 0.0)).astype(BF16)
        first = pltpu.make_async_copy(grad_box, kept_grad.at[:, position], sems.at[1])
        first.start()
        put_shifts(pieces, grad_conv.astype(BF16).astype(F32), side, side, rows)
        back = conv_of(pieces, weight, -1, side, rows)
        out[...] = (pack[pl.ds(position, 1), :] * boost * back).astype(BF16)
        first.wait()


GROUP_BITS = 2
GROUP = 1 << GROUP_BITS


def pack_kernel(micro, side, count, kept_grad, *rest):
    outs, turned = rest[:GROUP], rest[GROUP]
    channels = kept_grad.shape[3]
    rows = side * micro * side
    part = channels // count
    here = lax.axis_index("dp")
    extra = micro * side
    stacked = kept_grad[...].reshape(rows + extra, channels).astype(F32)
    stacked = jnp.concatenate([stacked, jnp.zeros((128 - extra, channels), F32)], axis=0)
    turned[...] = jnp.transpose(stacked).astype(BF16)
    for flip in range(GROUP):
        for slot in range(count // GROUP):
            source = pl.multiple_of((here ^ flip ^ (slot << GROUP_BITS)) * part, part)
            outs[flip][pl.ds(slot * part, part), :] = turned[pl.ds(source, part), :]


def weight_grad_kernel(micro, side, count, chunks, *refs):
    grads, mods, weight = refs[:GROUP], refs[GROUP : 2 * GROUP], refs[2 * GROUP]
    refs = refs[2 * GROUP + 1 :]
    outs, (pieces, mixture) = refs[: 2 * len(chunks)], refs[2 * len(chunks) :]
    channels = weight.shape[1]
    rows = side * micro * side
    band = micro * side
    tall = rows + 2 * band
    part = channels // count
    here = lax.axis_index("dp")
    blank = jnp.zeros((band, channels), BF16)
    for member in range(GROUP):
        base = member * tall
        for index in range(3):
            pieces[index, pl.ds(base, band), :] = blank
            pieces[index, pl.ds(base + band + rows, band), :] = blank
        value = mods[member][pl.ds(0, side)].reshape(rows, channels)
        put_shifts(pieces, value.astype(F32), side, base + band, rows)
        terms = grads[member][:, pl.ds(rows, 128)].astype(F32)
        squares = mods[member][side].reshape(band, channels).astype(F32)
        left = lax.broadcasted_iota(jnp.int32, (128, 128), 0)
        right = lax.broadcasted_iota(jnp.int32, (128, 128), 1)
        join = ((left // side == right) & (left % side < 2) & (right < micro)).astype(F32)
        terms = jnp.dot(terms, join, preferred_element_type=F32, precision=lax.Precision.HIGHEST)
        joined = lax.broadcasted_iota(jnp.int32, (8, band), 0) == lax.broadcasted_iota(
            jnp.int32, (8, band), 1
        ) // side
        squares = jnp.dot(joined.astype(F32), squares, preferred_element_type=F32, precision=lax.Precision.HIGHEST)
        term = jnp.dot(
            terms[:, :8], squares, preferred_element_type=F32, precision=lax.Precision.HIGHEST
        )
        if member:
            mixture[...] += term
        else:
            mixture[...] = term
    slots = count // GROUP
    for chunk, taps in enumerate(chunks):
        keep, send = outs[2 * chunk], outs[2 * chunk + 1]
        for spot, tap in enumerate(taps):
            total = None
            for member in range(GROUP):
                begin = member * tall + (tap // 3) * band
                term = jnp.dot(
                    grads[member][:, pl.ds(0, rows)], pieces[tap % 3, pl.ds(begin, rows), :],
                    preferred_element_type=F32,
                )
                total = term if total is None else total + term
            for slot in range(slots):
                source = pl.multiple_of((here ^ (slot << GROUP_BITS)) * part, part)
                fixed = total[slot * part : (slot + 1) * part] - weight[
                    pl.ds(tap * channels + source, part), :
                ].astype(F32) * mixture[pl.ds(slot * part, part), :]
                if slot < slots // 2:
                    keep[slot, spot] = fixed
                else:
                    send[slot - slots // 2, spot] = fixed.astype(BF16)


def on_device(
    text_ids, seed_ids, text_table, latent_table, start_map, style_weight, conv_weight, score_head
):
    sections = lax.axis_size("section")
    count = lax.axis_size("dp")
    bits = count.bit_length() - 1
    gen_count = sections - sections // 4
    section_at = lax.axis_index("section")
    here = lax.axis_index("dp")
    is_gen = section_at < gen_count
    micro = seed_ids.shape[0]
    channels, pixels = start_map.shape
    side = RES
    vocab_rows = text_table.shape[0]
    norm_div = pixels * math.sqrt(channels)

    ids = text_ids[None]
    weight = conv_weight[0]
    weight_out = jnp.transpose(weight, (1, 0, 2))
    flat_out = weight_out.reshape(9 * channels, channels)
    squares = jnp.sum(jnp.square(weight_out.astype(F32)), axis=0)
    first_map = start_map.T
    latent = jnp.take(latent_table, seed_ids, axis=0)
    for stage in range(bits):
        other = swap(ids, 1 << stage, count)
        if stage == 0:
            other, squares, first_map, latent = lax.optimization_barrier(
                (other, squares, first_map, latent)
            )
        ids = jnp.concatenate([ids, other], axis=0)
    wanted = ids.reshape(count * micro, TXT_LEN) - here * vocab_rows
    rows = lax.broadcasted_iota(jnp.int32, (1, 1, vocab_rows), 2)
    hits = jnp.sum((wanted[:, :, None] == rows).astype(F32), axis=1)
    sums = jnp.dot(hits.astype(BF16), text_table, preferred_element_type=F32)
    sums = sums.reshape(count, micro, channels)
    for stage in reversed(range(bits)):
        half = 1 << stage
        sums = sums[:half] + swap(sums[half:], half, count)
    text_mean = sums[0] / TXT_LEN

    code_now = jnp.where(is_gen, latent + text_mean, text_mean).astype(BF16)
    styles = 1.0 + lax.dot_general(
        code_now, style_weight[0], (((1,), (1,)), ((), ())), preferred_element_type=F32
    )
    demods = lax.rsqrt(
        lax.dot_general(
            styles * styles, squares, (((1,), (1,)), ((), ())), precision=lax.Precision.HIGHEST
        )
        + 1e-08
    )
    demods = jnp.where(is_gen, demods, jnp.ones_like(demods))
    rest = ((0, 8 - micro), (0, 0))
    pack = jnp.concatenate([jnp.pad(styles, rest), jnp.pad(demods, rest)], axis=0)
    head = score_head[None]
    ticks = micro + sections - 1

    whole = pl.BlockSpec(memory_space=VMEM)
    far = pl.BlockSpec(memory_space=pltpu.HBM)
    flops = 2 * 9 * channels * channels * pixels
    conv_cost = pl.CostEstimate(
        flops=flops, bytes_accessed=9 * channels * channels * 2 + 5 * channels * pixels * 2,
        transcendentals=channels * pixels,
    )
    tall = 2 * side + pixels
    conv_scratch = [VMEM((3, tall, channels), BF16)]
    plain = jax.ShapeDtypeStruct((pixels, channels), BF16)
    lined = jax.ShapeDtypeStruct((side + 1, micro, side, channels), BF16)
    tower = jax.ShapeDtypeStruct((SLOTS, pixels, channels), F32)

    def forward(tick, arrays):
        return pl.pallas_call(
            functools.partial(forward_kernel, tick, side, micro),
            in_specs=[whole] * 5 + [far] * 2 if tick else [whole] * 4,
            out_specs=[whole, far, far, whole],
            out_shape=[plain, lined, tower, jax.ShapeDtypeStruct((8, 128), F32)],
            scratch_shapes=conv_scratch
            + [
                VMEM((side + 1, side, channels), BF16),
                VMEM((pixels, channels), F32),
                pltpu.SemaphoreType.DMA((2,)),
            ],
            input_output_aliases={5: 1, 6: 2} if tick else {},
            cost_estimate=conv_cost,
            compiler_params=params(),
            name="forward_conv",
        )(*arrays)

    def backward(tick, arrays):
        fixed = 3 + micro if tick else 2 + micro
        return pl.pallas_call(
            functools.partial(backward_kernel, tick, side, micro, norm_div),
            in_specs=[whole] * fixed + [far, whole] + [far] * (1 if tick else 0),
            out_specs=[whole, far],
            out_shape=[plain, lined],
            scratch_shapes=conv_scratch
            + [
                VMEM((pixels, channels), F32),
                VMEM((side + 1, side, channels), BF16),
                pltpu.SemaphoreType.DMA((2,)),
            ],
            input_output_aliases={fixed + 2: 1} if tick else {},
            cost_estimate=conv_cost,
            compiler_params=params(),
            name="backward_conv",
        )(*arrays)

    scores = []
    kept_in = kept_conv = outgoing = None
    for tick in range(ticks):
        if tick:
            received = lax.ppermute(
                outgoing, "section", [(i, i + 1) for i in range(sections - 1) if 0 <= tick - 1 - i < micro]
            )
            arrays = (received, first_map, pack, head, flat_out, kept_in, kept_conv)
        else:
            arrays = (first_map, pack, head, flat_out)
        outgoing, kept_in, kept_conv, score = forward(tick, arrays)
        scores.append(score)
    scores = scores[sections - 1 :]
    for hop in range(sections - gen_count - 1):
        target = sections - 2 - hop
        passed = lax.ppermute(scores, "section", [(target + 1, target)])
        scores = [jnp.where(section_at == target, new, old) for new, old in zip(passed, scores)]

    mods = [kept_in]
    for flip in range(1, GROUP):
        mods.append(swap(kept_in, flip, count))
    kept_grad = outgoing = None
    for tick in range(ticks):
        arrays = (head, pack, *scores, kept_conv, flat_out)
        if tick:
            received = lax.ppermute(
                outgoing, "section",
                [(i, i - 1) for i in range(1, sections) if 0 <= tick - 1 - (sections - 1 - i) < micro],
            )
            arrays = (received, *arrays, kept_grad)
        outgoing, kept_grad = backward(tick, arrays)

    part = channels // count
    own = channels // GROUP
    chunks = ((0, 1, 2), (3, 4, 5), (6, 7, 8))
    wide = micro * pixels + 128
    packed = pl.pallas_call(
        functools.partial(pack_kernel, micro, side, count),
        in_specs=[whole],
        out_specs=[whole] * GROUP,
        out_shape=[jax.ShapeDtypeStruct((own, wide), BF16)] * GROUP,
        scratch_shapes=[VMEM((channels, wide), BF16)],
        cost_estimate=pl.CostEstimate(flops=0, bytes_accessed=4 * micro * pixels * channels, transcendentals=0),
        compiler_params=params(),
        name="pack_grad",
    )(kept_grad)
    grads = [packed[0]] + [swap(packed[flip], flip, count) for flip in range(1, GROUP)]
    slots = count // GROUP
    shapes = []
    for taps in chunks:
        shapes += [
            jax.ShapeDtypeStruct((slots // 2, len(taps), part, channels), F32),
            jax.ShapeDtypeStruct((slots // 2, len(taps), part, channels), BF16),
        ]
    pairs = pl.pallas_call(
        functools.partial(weight_grad_kernel, micro, side, count, chunks),
        in_specs=[whole] * (2 * GROUP + 1),
        out_specs=[whole] * len(shapes),
        out_shape=shapes,
        scratch_shapes=[VMEM((3, GROUP * micro * tall, channels), BF16), VMEM((own, channels), F32)],
        cost_estimate=pl.CostEstimate(flops=micro * flops, bytes_accessed=20 * 1024 * 1024, transcendentals=0),
        compiler_params=params(),
        name="weight_grad",
    )(*grads, *mods, flat_out)
    done = [None] * 9
    for chunk, taps in enumerate(chunks):
        keep, send = pairs[2 * chunk], pairs[2 * chunk + 1]
        half = slots // 2
        while True:
            total = keep + swap(send, half << GROUP_BITS, count).astype(F32)
            half //= 2
            if not half:
                break
            keep = total[:half]
            send = total[half:].astype(BF16)
        for spot, tap in enumerate(taps):
            done[tap] = total[0, spot]
    return jnp.stack(done, axis=1)[None]


def solution(mesh):
    placed = (
        P("dp", None),
        P("dp"),
        P("dp", None),
        P(),
        P(),
        P("section", None, None),
        P("section", None, None, None),
        P(),
    )
    return jax.shard_map(
        on_device,
        mesh=mesh,
        in_specs=placed,
        out_specs=P("section", "dp", None, None),
        check_vma=False,
    )
```

```python
import functools
import math

import jax
import jax.numpy as jnp
from jax import lax
from jax.experimental import pallas as pl
from jax.experimental.pallas import tpu as pltpu
from jax.sharding import PartitionSpec as P


TXT_LEN = 77
RES = 16
F32 = jnp.float32
BF16 = jnp.bfloat16
VMEM = pltpu.VMEM
LIMIT = 32 * 1024 * 1024


def params():
    return pltpu.CompilerParams(vmem_limit_bytes=LIMIT)


def swap(x, bit, count):
    return lax.ppermute(x, "dp", [(i, i ^ bit) for i in range(count)])


def column_masks(rows, side):
    column = lax.broadcasted_iota(jnp.int32, (rows, 1), 0) % side
    return column != 0, column != side - 1


def put_shifts(pieces, value, side, at, rows):
    not_first, not_last = column_masks(rows, side)
    left = jnp.where(not_first, pltpu.roll(value, 1, 0), 0.0)
    right = jnp.where(not_last, pltpu.roll(value, rows - 1, 0), 0.0)
    for index, shifted in enumerate((left, value, right)):
        pieces[index, pl.ds(at, rows), :] = shifted.astype(BF16)


def blank_edges(pieces, rows, pad):
    blank = jnp.zeros((pad, pieces.shape[2]), BF16)
    for index in range(3):
        pieces[index, pl.ds(0, pad), :] = blank
        pieces[index, pl.ds(pad + rows, pad), :] = blank


def conv_of(pieces, weight, sign, side, rows):
    channels = pieces.shape[2]
    total = None
    for tap in range(9):
        down, across = sign * (tap // 3 - 1), sign * (tap % 3 - 1)
        term = lax.dot_general(
            pieces[across + 1, pl.ds(side + down * side, rows), :],
            weight[pl.ds(tap * channels, channels), :],
            (((1,), ((1 if sign > 0 else 0),)), ((), ())),
            preferred_element_type=F32,
        )
        total = term if total is None else total + term
    return total


def prepare_kernel(latent_in, weight, start, squares, first_map, latent):
    channels = weight.shape[1]
    latent[...] = latent_in[...]
    for block in range(0, channels, 64):
        total = None
        for tap in range(9):
            value = weight[pl.ds(tap * channels + block, 64), :].astype(F32)
            total = value * value if total is None else total + value * value
        squares[pl.ds(block, 64), :] = total
    first_map[...] = jnp.transpose(start[...].astype(F32)).astype(BF16)


def join_kernel(*refs):
    out = refs[-1]
    size = refs[0].shape[0]
    for index, ref in enumerate(refs[:-1]):
        out[pl.ds(index * size, size), :] = ref[...]


def text_kernel(ids, other_ids, table, stay, go):
    vocab_rows = table.shape[0]
    here = lax.axis_index("dp")
    half = ids.shape[0]
    full = vocab_rows // 128 * 128
    width = full if full == vocab_rows else full + 128
    row = lax.broadcasted_iota(jnp.int32, (2 * half, width), 1)
    row = jnp.where(row < vocab_rows, row + here * vocab_rows, -1)
    wanted = jnp.concatenate([ids[...], other_ids[...]], axis=0)
    hits = jnp.zeros((2 * half, width), F32)
    for token in range(TXT_LEN):
        hits = hits + jnp.where(wanted[:, token : token + 1] == row, 1.0, 0.0)
    hits = hits.astype(BF16)
    sums = jnp.dot(hits[:, :full], table[pl.ds(0, full), :], preferred_element_type=F32)
    if width > full:
        last = table[pl.ds(full, vocab_rows - full), :].astype(F32)
        blank = jnp.zeros((width - vocab_rows, table.shape[1]), F32)
        last = jnp.concatenate([last, blank], axis=0).astype(BF16)
        sums = sums + jnp.dot(hits[:, full:], last, preferred_element_type=F32)
    stay[...] = sums[:half]
    go[...] = sums[half:]


def add_kernel(one, two, *outs):
    total = one[...] + two[...]
    size = outs[0].shape[0]
    for index, out in enumerate(outs):
        out[...] = total[index * size : (index + 1) * size]


def style_kernel(*refs):
    sums, (latent, style_weight, squares, pack) = refs[:GROUP], refs[GROUP:]
    section = lax.axis_index("section")
    sections = lax.axis_size("section")
    is_gen = section < sections - sections // 4
    micro, channels = latent.shape
    text_mean = ((sums[0][...] + sums[1][...]) + (sums[2][...] + sums[3][...])) / TXT_LEN
    code = jnp.where(is_gen, latent[...] + text_mean, text_mean)
    code = jnp.concatenate([code, jnp.zeros((8 - micro, channels), F32)], axis=0).astype(BF16)
    across = (((1,), (1,)), ((), ()))
    styles = 1.0 + lax.dot_general(code, style_weight[...], across, preferred_element_type=F32)
    norms = lax.dot_general(
        styles * styles, squares[...], across, preferred_element_type=F32,
        precision=lax.Precision.HIGHEST,
    )
    pack[pl.ds(0, 8), :] = styles
    pack[pl.ds(8, 8), :] = jnp.where(is_gen, lax.rsqrt(norms + 1e-08), 1.0)


def forward_kernel(tick, side, micro, *refs):
    if tick:
        received, start, pack, head, weight = refs[:5]
        refs = refs[7:]
    else:
        start, pack, head, weight = refs[:4]
        received = start
        refs = refs[4:]
    out, kept_in, kept_conv, score, pieces, mod_box, conv_box, sems = refs
    rows = start.shape[0]
    section = lax.axis_index("section")
    position = tick - section

    @pl.when((position >= 0) & (position < micro))
    def _():
        blank_edges(pieces, rows, side)
        style = pack[pl.ds(position, 1), :]
        source = received[...]
        if tick:
            source = jnp.where(section == 0, start[...].astype(F32), source.astype(F32))
        mod = (style * source.astype(F32)).astype(BF16)
        mod_box[pl.ds(0, side)] = mod.reshape(side, side, mod.shape[1])
        squared = style * style
        high = squared.astype(BF16).astype(F32)
        row = lax.broadcasted_iota(jnp.int32, (side, mod.shape[1]), 0)
        low = jnp.where(row < 4, squared - high, 0.0)
        mod_box[side] = jnp.where(row < 2, high, low).astype(BF16)
        first = pltpu.make_async_copy(mod_box, kept_in.at[:, position], sems.at[0])
        first.start()
        put_shifts(pieces, mod.astype(F32), side, side, rows)
        conv = conv_of(pieces, weight, 1, side, rows)
        conv_box[...] = conv
        second = pltpu.make_async_copy(conv_box, kept_conv.at[position], sems.at[1])
        second.start()
        pre = pack[pl.ds(8 + position, 1), :] * conv
        result = (pre / (1.0 + jnp.exp(-pre))).astype(BF16)
        out[...] = result
        sums = jnp.sum(result.astype(F32), axis=0, keepdims=True) * head[...]
        score[...] = jnp.broadcast_to(jnp.sum(sums, axis=1, keepdims=True), score.shape)
        first.wait()
        second.wait()


def backward_kernel(tick, side, micro, norm_div, *refs):
    if tick:
        received = refs[0]
        refs = refs[1:]
    head, pack = refs[:2]
    scores, refs = refs[2 : 2 + micro], refs[2 + micro :]
    kept_conv, weight = refs[:2]
    refs = refs[3:] if tick else refs[2:]
    out, kept_grad, pieces, conv_box, grad_box, sems = refs
    rows = conv_box.shape[0]
    section = lax.axis_index("section")
    sections = lax.axis_size("section")
    gen_count = sections - sections // 4
    position = tick - (sections - 1 - section)

    @pl.when((position >= 0) & (position < micro))
    def _():
        load = pltpu.make_async_copy(kept_conv.at[position], conv_box, sems.at[0])
        load.start()
        blank_edges(pieces, rows, side)
        raw = scores[0][...]
        for index in range(1, micro):
            raw = jnp.where(position == index, scores[index][...], raw)
        raw = raw[:1, :1] / norm_div
        d_factor = (1.0 / (1.0 + jnp.exp(-raw))).astype(BF16).astype(F32)
        g_factor = (-1.0 / (1.0 + jnp.exp(raw))).astype(BF16).astype(F32)
        scale = jnp.where(section < gen_count, jnp.ones_like(raw), d_factor)
        boost = jnp.where(section == gen_count, g_factor, jnp.ones_like(raw))
        demod = pack[pl.ds(8 + position, 1), :]
        unit = (head[...] / norm_div).astype(BF16).astype(F32)
        incoming = jnp.broadcast_to(unit, conv_box.shape)
        if tick:
            incoming = jnp.where(section == sections - 1, incoming, received[...].astype(F32))
        load.wait()
        conv = conv_box[...]
        pre = demod * conv
        sigma = 1.0 / (1.0 + jnp.exp(-pre))
        grad_pre = incoming * sigma * (1.0 + pre * (1.0 - sigma))
        grad_conv = demod * grad_pre
        channels = conv.shape[1]
        grad_box[pl.ds(0, side)] = (scale * grad_conv).astype(BF16).reshape(side, side, channels)
        term = jnp.sum(grad_pre * conv, axis=0, keepdims=True) * demod * demod * demod
        term = jnp.where(section < gen_count, term, 0.0)
        high = term.astype(BF16).astype(F32)
        row = lax.broadcasted_iota(jnp.int32, (side, channels), 0)
        both = jnp.where(row % 2 == 0, high, term - high)
        grad_box[side] = jnp.where(row < 4, both, 0.0).astype(BF16)
        first = pltpu.make_async_copy(grad_box, kept_grad.at[:, position], sems.at[1])
        first.start()
        put_shifts(pieces, grad_conv.astype(BF16).astype(F32), side, side, rows)
        back = conv_of(pieces, weight, -1, side, rows)
        out[...] = (pack[pl.ds(position, 1), :] * boost * back).astype(BF16)
        first.wait()


GROUP_BITS = 2
GROUP = 1 << GROUP_BITS


def pack_kernel(micro, side, count, kept_grad, *rest):
    outs, turned = rest[:GROUP], rest[GROUP]
    channels = kept_grad.shape[3]
    rows = side * micro * side
    part = channels // count
    here = lax.axis_index("dp")
    extra = micro * side
    stacked = kept_grad[...].reshape(rows + extra, channels).astype(F32)
    stacked = jnp.concatenate([stacked, jnp.zeros((128 - extra, channels), F32)], axis=0)
    turned[...] = jnp.transpose(stacked).astype(BF16)
    for flip in range(GROUP):
        for slot in range(count // GROUP):
            source = pl.multiple_of((here ^ flip ^ (slot << GROUP_BITS)) * part, part)
            outs[flip][pl.ds(slot * part, part), :] = turned[pl.ds(source, part), :]


def shift_kernel(micro, side, *refs):
    mods, pieces = refs[:GROUP], refs[GROUP]
    channels = pieces.shape[2]
    rows = side * micro * side
    band = micro * side
    blank = jnp.zeros((band, channels), BF16)
    for member in range(GROUP):
        base = member * (rows + 2 * band)
        for index in range(3):
            pieces[index, pl.ds(base, band), :] = blank
            pieces[index, pl.ds(base + band + rows, band), :] = blank
        value = mods[member][pl.ds(0, side)].reshape(rows, channels)
        put_shifts(pieces, value.astype(F32), side, base + band, rows)


def weight_grad_kernel(micro, side, count, taps, *refs):
    grads, mods = refs[:GROUP], refs[GROUP : 2 * GROUP]
    pieces, weight, keep, send = refs[2 * GROUP :]
    channels = weight.shape[1]
    rows = side * micro * side
    band = micro * side
    tall = rows + 2 * band
    part = channels // count
    here = lax.axis_index("dp")
    slots = count // GROUP
    mixture = None
    for member in range(GROUP):
        squared = mods[member][side].reshape(band, channels).astype(F32)
        squared = jnp.concatenate([squared, jnp.zeros((128 - band, channels), F32)], axis=0)
        term = jnp.dot(
            grads[member][:, pl.ds(rows, 128)], squared.astype(BF16), preferred_element_type=F32
        )
        mixture = term if mixture is None else mixture + term
    for spot, tap in enumerate(taps):
        total = None
        for member in range(GROUP):
            begin = member * tall + (tap // 3) * band
            term = jnp.dot(
                grads[member][:, pl.ds(0, rows)], pieces[tap % 3, pl.ds(begin, rows), :],
                preferred_element_type=F32,
            )
            total = term if total is None else total + term
        for slot in range(slots):
            source = pl.multiple_of((here ^ (slot << GROUP_BITS)) * part, part)
            fixed = total[slot * part : (slot + 1) * part] - weight[
                pl.ds(tap * channels + source, part), :
            ].astype(F32) * mixture[slot * part : (slot + 1) * part]
            if slot < slots // 2:
                keep[slot, spot] = fixed
            else:
                send[slot - slots // 2, spot] = fixed.astype(BF16)


def on_device(
    text_ids, seed_ids, text_table, latent_table, start_map, style_weight, conv_weight, score_head
):
    sections = lax.axis_size("section")
    count = lax.axis_size("dp")
    bits = count.bit_length() - 1
    gen_count = sections - sections // 4
    section_at = lax.axis_index("section")
    micro = seed_ids.shape[0]
    channels, pixels = start_map.shape
    side = RES
    norm_div = pixels * math.sqrt(channels)

    whole = pl.BlockSpec(memory_space=VMEM)
    far = pl.BlockSpec(memory_space=pltpu.HBM)
    flat_out = jnp.transpose(conv_weight[0], (1, 0, 2)).reshape(9 * channels, channels)

    def small(kernel, shapes, *arrays, specs=None, scratch=()):
        return pl.pallas_call(
            kernel,
            in_specs=specs or [whole] * len(arrays),
            out_specs=[whole] * len(shapes),
            out_shape=[jax.ShapeDtypeStruct(*shape) for shape in shapes],
            scratch_shapes=scratch,
            compiler_params=params(),
        )(*arrays)

    parts = [text_ids]
    for flip in range(1, GROUP):
        parts.append(swap(text_ids, flip, count))
    squares, first_map, latent = small(
        prepare_kernel,
        [((channels, channels), F32), ((pixels, channels), BF16), ((micro, channels), F32)],
        jnp.take(latent_table, seed_ids, axis=0), flat_out, start_map,
    )
    (ids,) = small(join_kernel, [((GROUP * micro, TXT_LEN), jnp.int32)], *parts)
    for stage in range(GROUP_BITS, bits):
        other_ids = swap(ids, 1 << stage, count)
        if stage < bits - 1:
            (ids,) = small(join_kernel, [((2 * ids.shape[0], TXT_LEN), jnp.int32)], ids, other_ids)
    half = count * micro // 2
    stay, go = small(text_kernel, [((half, channels), F32)] * 2, ids, other_ids, text_table)
    for stage in reversed(range(GROUP_BITS, bits)):
        got = swap(go, 1 << stage, count)
        size, outs = (micro, GROUP) if stage == GROUP_BITS else (half // 2, 2)
        sums = small(add_kernel, [((size, channels), F32)] * outs, stay, got)
        if stage > GROUP_BITS:
            stay, go = sums
            half //= 2
    sums = [sums[0]] + [swap(sums[flip], flip, count) for flip in range(1, GROUP)]
    (pack,) = small(style_kernel, [((16, channels), F32)], *sums, latent, style_weight[0], squares)
    head = score_head[None]
    ticks = micro + sections - 1

    flops = 2 * 9 * channels * channels * pixels
    conv_cost = pl.CostEstimate(
        flops=flops, bytes_accessed=9 * channels * channels * 2 + 5 * channels * pixels * 2,
        transcendentals=channels * pixels,
    )
    tall = 2 * side + pixels
    conv_scratch = [VMEM((3, tall, channels), BF16)]
    plain = jax.ShapeDtypeStruct((pixels, channels), BF16)
    lined = jax.ShapeDtypeStruct((side + 1, micro, side, channels), BF16)
    tower = jax.ShapeDtypeStruct((micro, pixels, channels), F32)

    def forward(tick, arrays):
        return pl.pallas_call(
            functools.partial(forward_kernel, tick, side, micro),
            in_specs=[whole] * 5 + [far] * 2 if tick else [whole] * 4,
            out_specs=[whole, far, far, whole],
            out_shape=[plain, lined, tower, jax.ShapeDtypeStruct((8, 128), F32)],
            scratch_shapes=conv_scratch
            + [
                VMEM((side + 1, side, channels), BF16),
                VMEM((pixels, channels), F32),
                pltpu.SemaphoreType.DMA((2,)),
            ],
            input_output_aliases={5: 1, 6: 2} if tick else {},
            cost_estimate=conv_cost,
            compiler_params=params(),
            name="forward_conv",
        )(*arrays)

    def backward(tick, arrays):
        fixed = 3 + micro if tick else 2 + micro
        return pl.pallas_call(
            functools.partial(backward_kernel, tick, side, micro, norm_div),
            in_specs=[whole] * fixed + [far, whole] + [far] * (1 if tick else 0),
            out_specs=[whole, far],
            out_shape=[plain, lined],
            scratch_shapes=conv_scratch
            + [
                VMEM((pixels, channels), F32),
                VMEM((side + 1, side, channels), BF16),
                pltpu.SemaphoreType.DMA((2,)),
            ],
            input_output_aliases={fixed + 2: 1} if tick else {},
            cost_estimate=conv_cost,
            compiler_params=params(),
            name="backward_conv",
        )(*arrays)

    scores = []
    kept_in = kept_conv = outgoing = None
    for tick in range(ticks):
        if tick:
            received = lax.ppermute(
                outgoing, "section", [(i, i + 1) for i in range(sections - 1) if 0 <= tick - 1 - i < micro]
            )
            arrays = (received, first_map, pack, head, flat_out, kept_in, kept_conv)
        else:
            arrays = (first_map, pack, head, flat_out)
        outgoing, kept_in, kept_conv, score = forward(tick, arrays)
        scores.append(score)
    scores = scores[sections - 1 :]
    for hop in range(sections - gen_count - 1):
        target = sections - 2 - hop
        passed = lax.ppermute(scores, "section", [(target + 1, target)])
        scores = [jnp.where(section_at == target, new, old) for new, old in zip(passed, scores)]

    mods = [kept_in]
    for flip in range(1, GROUP):
        mods.append(swap(kept_in, flip, count))
    kept_grad = outgoing = None
    for tick in range(ticks):
        arrays = (head, pack, *scores, kept_conv, flat_out)
        if tick:
            received = lax.ppermute(
                outgoing, "section",
                [(i, i - 1) for i in range(1, sections) if 0 <= tick - 1 - (sections - 1 - i) < micro],
            )
            arrays = (received, *arrays, kept_grad)
        outgoing, kept_grad = backward(tick, arrays)

    part = channels // count
    own = channels // GROUP
    chunks = ((0, 1, 2), (3, 4, 5), (6, 7, 8))
    wide = micro * pixels + 128
    packed = pl.pallas_call(
        functools.partial(pack_kernel, micro, side, count),
        in_specs=[whole],
        out_specs=[whole] * GROUP,
        out_shape=[jax.ShapeDtypeStruct((own, wide), BF16)] * GROUP,
        scratch_shapes=[VMEM((channels, wide), BF16)],
        cost_estimate=pl.CostEstimate(flops=0, bytes_accessed=4 * micro * pixels * channels, transcendentals=0),
        compiler_params=params(),
        name="pack_grad",
    )(kept_grad)
    grads = [packed[0]]
    for flip in range(1, GROUP):
        grads.append(swap(packed[flip], flip, count))
    slots = count // GROUP
    pieces = pl.pallas_call(
        functools.partial(shift_kernel, micro, side),
        in_specs=[whole] * GROUP,
        out_specs=whole,
        out_shape=jax.ShapeDtypeStruct((3, GROUP * micro * tall, channels), BF16),
        cost_estimate=pl.CostEstimate(flops=0, bytes_accessed=16 * 1024 * 1024, transcendentals=0),
        compiler_params=params(),
        name="shift",
    )(*mods)
    pairs = []
    for taps in chunks:
        pairs += pl.pallas_call(
            functools.partial(weight_grad_kernel, micro, side, count, taps),
            in_specs=[whole] * (2 * GROUP + 2),
            out_specs=[whole] * 2,
            out_shape=[
                jax.ShapeDtypeStruct((slots // 2, len(taps), part, channels), F32),
                jax.ShapeDtypeStruct((slots // 2, len(taps), part, channels), BF16),
            ],
            cost_estimate=pl.CostEstimate(
                flops=micro * flops // len(chunks), bytes_accessed=5 * 1024 * 1024, transcendentals=0
            ),
            compiler_params=params(),
            name="weight_grad",
        )(*grads, *mods, pieces, flat_out)
    done = [None] * 9
    for chunk, taps in enumerate(chunks):
        keep, send = pairs[2 * chunk], pairs[2 * chunk + 1]
        half = slots // 2
        while True:
            total = keep + swap(send, half << GROUP_BITS, count).astype(F32)
            half //= 2
            if not half:
                break
            keep = total[:half]
            send = total[half:].astype(BF16)
        for spot, tap in enumerate(taps):
            done[tap] = total[0, spot]
    return jnp.stack(done, axis=1)[None]


def solution(mesh):
    placed = (
        P("dp", None),
        P("dp"),
        P("dp", None),
        P(),
        P(),
        P("section", None, None),
        P("section", None, None, None),
        P(),
    )
    return jax.shard_map(
        on_device,
        mesh=mesh,
        in_specs=placed,
        out_specs=P("section", "dp", None, None),
        check_vma=False,
    )
```

```python
import functools
import math

import jax
import jax.numpy as jnp
from jax import lax
from jax.experimental import pallas as pl
from jax.experimental.pallas import tpu as pltpu
from jax.sharding import PartitionSpec as P


TXT_LEN = 77
RES = 16
F32 = jnp.float32
BF16 = jnp.bfloat16
VMEM = pltpu.VMEM
LIMIT = 32 * 1024 * 1024


def params():
    return pltpu.CompilerParams(vmem_limit_bytes=LIMIT)


def swap(x, bit, count):
    return lax.ppermute(x, "dp", [(i, i ^ bit) for i in range(count)])


def device_flip(value, odd):
    if odd:
        return value
    low, high = value & 1, (value >> 2) & 1
    return (value & ~5) | (low << 2) | high


def own_flip(value, section):
    return jnp.where(section % 2 == 1, device_flip(value, 1), device_flip(value, 0))


def group_swap(x, value, sections, count):
    pairs = []
    for section in range(sections):
        flip = device_flip(value, section % 2)
        pairs += [(section * count + i, section * count + (i ^ flip)) for i in range(count)]
    return lax.ppermute(x, ("section", "dp"), pairs)


def column_masks(rows, side):
    column = lax.broadcasted_iota(jnp.int32, (rows, 1), 0) % side
    return column != 0, column != side - 1


def put_shifts(pieces, value, side, at, rows):
    not_first, not_last = column_masks(rows, side)
    left = jnp.where(not_first, pltpu.roll(value, 1, 0), 0.0)
    right = jnp.where(not_last, pltpu.roll(value, rows - 1, 0), 0.0)
    for index, shifted in enumerate((left, value, right)):
        pieces[index, pl.ds(at, rows), :] = shifted.astype(BF16)


def blank_edges(pieces, rows, pad):
    blank = jnp.zeros((pad, pieces.shape[2]), BF16)
    for index in range(3):
        pieces[index, pl.ds(0, pad), :] = blank
        pieces[index, pl.ds(pad + rows, pad), :] = blank


def conv_of(pieces, weight, sign, side, rows):
    channels = pieces.shape[2]
    total = None
    for tap in range(9):
        down, across = sign * (tap // 3 - 1), sign * (tap % 3 - 1)
        term = lax.dot_general(
            pieces[across + 1, pl.ds(side + down * side, rows), :],
            weight[pl.ds(tap * channels, channels), :],
            (((1,), ((1 if sign > 0 else 0),)), ((), ())),
            preferred_element_type=F32,
        )
        total = term if total is None else total + term
    return total


def prepare_kernel(latent_in, weight, start, squares, first_map, latent):
    channels = weight.shape[1]
    latent[...] = latent_in[...]
    for block in range(0, channels, 64):
        total = None
        for tap in range(9):
            value = weight[pl.ds(tap * channels + block, 64), :].astype(F32)
            total = value * value if total is None else total + value * value
        squares[pl.ds(block, 64), :] = total
    first_map[...] = jnp.transpose(start[...].astype(F32)).astype(BF16)


def join_kernel(*refs):
    out = refs[-1]
    size = refs[0].shape[0]
    for index, ref in enumerate(refs[:-1]):
        out[pl.ds(index * size, size), :] = ref[...]


def text_kernel(ids, other_ids, table, stay, go):
    vocab_rows = table.shape[0]
    here = lax.axis_index("dp")
    half = ids.shape[0]
    full = vocab_rows // 128 * 128
    width = full if full == vocab_rows else full + 128
    row = lax.broadcasted_iota(jnp.int32, (2 * half, width), 1)
    row = jnp.where(row < vocab_rows, row + here * vocab_rows, -1)
    wanted = jnp.concatenate([ids[...], other_ids[...]], axis=0)
    hits = jnp.zeros((2 * half, width), F32)
    for token in range(TXT_LEN):
        hits = hits + jnp.where(wanted[:, token : token + 1] == row, 1.0, 0.0)
    hits = hits.astype(BF16)
    sums = jnp.dot(hits[:, :full], table[pl.ds(0, full), :], preferred_element_type=F32)
    if width > full:
        last = table[pl.ds(full, vocab_rows - full), :].astype(F32)
        blank = jnp.zeros((width - vocab_rows, table.shape[1]), F32)
        last = jnp.concatenate([last, blank], axis=0).astype(BF16)
        sums = sums + jnp.dot(hits[:, full:], last, preferred_element_type=F32)
    stay[...] = sums[:half]
    go[...] = sums[half:]


def add_kernel(one, two, *outs):
    total = one[...] + two[...]
    size = outs[0].shape[0]
    for index, out in enumerate(outs):
        out[...] = total[index * size : (index + 1) * size]


def style_kernel(*refs):
    sums, (latent, style_weight, squares, pack) = refs[:GROUP], refs[GROUP:]
    section = lax.axis_index("section")
    sections = lax.axis_size("section")
    is_gen = section < sections - sections // 4
    micro, channels = latent.shape
    text_mean = ((sums[0][...] + sums[1][...]) + (sums[2][...] + sums[3][...])) / TXT_LEN
    code = jnp.where(is_gen, latent[...] + text_mean, text_mean)
    code = jnp.concatenate([code, jnp.zeros((8 - micro, channels), F32)], axis=0).astype(BF16)
    across = (((1,), (1,)), ((), ()))
    styles = 1.0 + lax.dot_general(code, style_weight[...], across, preferred_element_type=F32)
    norms = lax.dot_general(
        styles * styles, squares[...], across, preferred_element_type=F32,
        precision=lax.Precision.HIGHEST,
    )
    pack[pl.ds(0, 8), :] = styles
    pack[pl.ds(8, 8), :] = jnp.where(is_gen, lax.rsqrt(norms + 1e-08), 1.0)


def forward_kernel(tick, side, micro, *refs):
    if tick:
        from_core, from_chip, start, pack, head, weight = refs[:6]
        refs = refs[8:]
    else:
        start, pack, head, weight = refs[:4]
        refs = refs[4:]
    out, kept_in, kept_conv, score, pieces, mod_box, conv_box, sems = refs
    rows = start.shape[0]
    section = lax.axis_index("section")
    position = tick - section

    @pl.when((position >= 0) & (position < micro))
    def _():
        blank_edges(pieces, rows, side)
        style = pack[pl.ds(position, 1), :]
        source = start[...].astype(F32)
        if tick:
            other = jnp.where(section % 2 == 1, from_core[...].astype(F32), from_chip[...].astype(F32))
            source = jnp.where(section == 0, source, other)
        mod = (style * source).astype(BF16)
        mod_box[pl.ds(0, side)] = mod.reshape(side, side, mod.shape[1])
        squared = style * style
        high = squared.astype(BF16).astype(F32)
        row = lax.broadcasted_iota(jnp.int32, (side, mod.shape[1]), 0)
        low = jnp.where(row < 4, squared - high, 0.0)
        mod_box[side] = jnp.where(row < 2, high, low).astype(BF16)
        first = pltpu.make_async_copy(mod_box, kept_in.at[:, position], sems.at[0])
        first.start()
        put_shifts(pieces, mod.astype(F32), side, side, rows)
        conv = conv_of(pieces, weight, 1, side, rows)
        conv_box[...] = conv
        second = pltpu.make_async_copy(conv_box, kept_conv.at[position], sems.at[1])
        second.start()
        pre = pack[pl.ds(8 + position, 1), :] * conv
        result = (pre / (1.0 + jnp.exp(-pre))).astype(BF16)
        out[...] = result
        sums = jnp.sum(result.astype(F32), axis=0, keepdims=True) * head[...]
        score[...] = jnp.broadcast_to(jnp.sum(sums, axis=1, keepdims=True), score.shape)
        first.wait()
        second.wait()


def backward_kernel(tick, side, micro, norm_div, *refs):
    if tick:
        from_core, from_chip = refs[:2]
        refs = refs[2:]
    head, pack = refs[:2]
    scores, refs = refs[2 : 2 + micro], refs[2 + micro :]
    kept_conv, weight = refs[:2]
    refs = refs[3:] if tick else refs[2:]
    out, kept_grad, pieces, conv_box, grad_box, sems = refs
    rows = conv_box.shape[0]
    section = lax.axis_index("section")
    sections = lax.axis_size("section")
    gen_count = sections - sections // 4
    position = tick - (sections - 1 - section)

    @pl.when((position >= 0) & (position < micro))
    def _():
        load = pltpu.make_async_copy(kept_conv.at[position], conv_box, sems.at[0])
        load.start()
        blank_edges(pieces, rows, side)
        raw = scores[0][...]
        for index in range(1, micro):
            raw = jnp.where(position == index, scores[index][...], raw)
        raw = raw[:1, :1] / norm_div
        d_factor = (1.0 / (1.0 + jnp.exp(-raw))).astype(BF16).astype(F32)
        g_factor = (-1.0 / (1.0 + jnp.exp(raw))).astype(BF16).astype(F32)
        scale = jnp.where(section < gen_count, jnp.ones_like(raw), d_factor)
        boost = jnp.where(section == gen_count, g_factor, jnp.ones_like(raw))
        demod = pack[pl.ds(8 + position, 1), :]
        unit = (head[...] / norm_div).astype(BF16).astype(F32)
        incoming = jnp.broadcast_to(unit, conv_box.shape)
        if tick:
            other = jnp.where(section % 2 == 0, from_core[...].astype(F32), from_chip[...].astype(F32))
            incoming = jnp.where(section == sections - 1, incoming, other)
        load.wait()
        conv = conv_box[...]
        pre = demod * conv
        sigma = 1.0 / (1.0 + jnp.exp(-pre))
        grad_pre = incoming * sigma * (1.0 + pre * (1.0 - sigma))
        grad_conv = demod * grad_pre
        channels = conv.shape[1]
        grad_box[pl.ds(0, side)] = (scale * grad_conv).astype(BF16).reshape(side, side, channels)
        term = jnp.sum(grad_pre * conv, axis=0, keepdims=True) * demod * demod * demod
        term = jnp.where(section < gen_count, term, 0.0)
        high = term.astype(BF16).astype(F32)
        row = lax.broadcasted_iota(jnp.int32, (side, channels), 0)
        both = jnp.where(row % 2 == 0, high, term - high)
        grad_box[side] = jnp.where(row < 4, both, 0.0).astype(BF16)
        first = pltpu.make_async_copy(grad_box, kept_grad.at[:, position], sems.at[1])
        first.start()
        put_shifts(pieces, grad_conv.astype(BF16).astype(F32), side, side, rows)
        back = conv_of(pieces, weight, -1, side, rows)
        out[...] = (pack[pl.ds(position, 1), :] * boost * back).astype(BF16)
        first.wait()


GROUP_BITS = 2
GROUP = 1 << GROUP_BITS


def pack_kernel(micro, side, count, kept_grad, *rest):
    outs, turned = rest[:GROUP], rest[GROUP]
    channels = kept_grad.shape[3]
    rows = side * micro * side
    part = channels // count
    here, section = lax.axis_index("dp"), lax.axis_index("section")
    extra = micro * side
    stacked = kept_grad[...].reshape(rows + extra, channels).astype(F32)
    stacked = jnp.concatenate([stacked, jnp.zeros((128 - extra, channels), F32)], axis=0)
    turned[...] = jnp.transpose(stacked).astype(BF16)
    for flip in range(GROUP):
        for slot in range(count // GROUP):
            block = here ^ own_flip(flip ^ (slot << GROUP_BITS), section)
            source = pl.multiple_of(block * part, part)
            outs[flip][pl.ds(slot * part, part), :] = turned[pl.ds(source, part), :]


def shift_kernel(micro, side, *refs):
    mods, pieces = refs[:GROUP], refs[GROUP]
    channels = pieces.shape[2]
    rows = side * micro * side
    band = micro * side
    blank = jnp.zeros((band, channels), BF16)
    for member in range(GROUP):
        base = member * (rows + 2 * band)
        for index in range(3):
            pieces[index, pl.ds(base, band), :] = blank
            pieces[index, pl.ds(base + band + rows, band), :] = blank
        value = mods[member][pl.ds(0, side)].reshape(rows, channels)
        put_shifts(pieces, value.astype(F32), side, base + band, rows)


def weight_grad_kernel(micro, side, count, taps, *refs):
    grads, mods = refs[:GROUP], refs[GROUP : 2 * GROUP]
    pieces, weight, keep, send = refs[2 * GROUP :]
    channels = weight.shape[1]
    rows = side * micro * side
    band = micro * side
    tall = rows + 2 * band
    part = channels // count
    here, section = lax.axis_index("dp"), lax.axis_index("section")
    slots = count // GROUP
    mixture = None
    for member in range(GROUP):
        squared = mods[member][side].reshape(band, channels).astype(F32)
        squared = jnp.concatenate([squared, jnp.zeros((128 - band, channels), F32)], axis=0)
        term = jnp.dot(
            grads[member][:, pl.ds(rows, 128)], squared.astype(BF16), preferred_element_type=F32
        )
        mixture = term if mixture is None else mixture + term
    for spot, tap in enumerate(taps):
        total = None
        for member in range(GROUP):
            begin = member * tall + (tap // 3) * band
            term = jnp.dot(
                grads[member][:, pl.ds(0, rows)], pieces[tap % 3, pl.ds(begin, rows), :],
                preferred_element_type=F32,
            )
            total = term if total is None else total + term
        for slot in range(slots):
            block = here ^ own_flip(slot << GROUP_BITS, section)
            source = pl.multiple_of(block * part, part)
            fixed = total[slot * part : (slot + 1) * part] - weight[
                pl.ds(tap * channels + source, part), :
            ].astype(F32) * mixture[slot * part : (slot + 1) * part]
            if slot < slots // 2:
                keep[slot, spot] = fixed
            else:
                send[slot - slots // 2, spot] = fixed.astype(BF16)


def on_device(
    text_ids, seed_ids, text_table, latent_table, start_map, style_weight, conv_weight, score_head
):
    sections = lax.axis_size("section")
    count = lax.axis_size("dp")
    bits = count.bit_length() - 1
    gen_count = sections - sections // 4
    section_at = lax.axis_index("section")
    micro = seed_ids.shape[0]
    channels, pixels = start_map.shape
    side = RES
    norm_div = pixels * math.sqrt(channels)

    whole = pl.BlockSpec(memory_space=VMEM)
    far = pl.BlockSpec(memory_space=pltpu.HBM)
    flat_out = jnp.transpose(conv_weight[0], (1, 0, 2)).reshape(9 * channels, channels)

    def small(kernel, shapes, *arrays, specs=None, scratch=()):
        return pl.pallas_call(
            kernel,
            in_specs=specs or [whole] * len(arrays),
            out_specs=[whole] * len(shapes),
            out_shape=[jax.ShapeDtypeStruct(*shape) for shape in shapes],
            scratch_shapes=scratch,
            compiler_params=params(),
        )(*arrays)

    parts = [text_ids]
    for flip in range(1, GROUP):
        parts.append(swap(text_ids, flip, count))
    squares, first_map, latent = small(
        prepare_kernel,
        [((channels, channels), F32), ((pixels, channels), BF16), ((micro, channels), F32)],
        jnp.take(latent_table, seed_ids, axis=0), flat_out, start_map,
    )
    (ids,) = small(join_kernel, [((GROUP * micro, TXT_LEN), jnp.int32)], *parts)
    for stage in range(GROUP_BITS, bits):
        other_ids = swap(ids, 1 << stage, count)
        if stage < bits - 1:
            (ids,) = small(join_kernel, [((2 * ids.shape[0], TXT_LEN), jnp.int32)], ids, other_ids)
    half = count * micro // 2
    stay, go = small(text_kernel, [((half, channels), F32)] * 2, ids, other_ids, text_table)
    for stage in reversed(range(GROUP_BITS, bits)):
        got = swap(go, 1 << stage, count)
        size, outs = (micro, GROUP) if stage == GROUP_BITS else (half // 2, 2)
        sums = small(add_kernel, [((size, channels), F32)] * outs, stay, got)
        if stage > GROUP_BITS:
            stay, go = sums
            half //= 2
    sums = list(sums)
    for flip in range(1, GROUP):
        sums[flip] = swap(sums[flip], flip, count)
    (pack,) = small(style_kernel, [((16, channels), F32)], *sums, latent, style_weight[0], squares)
    head = score_head[None]
    ticks = micro + sections - 1

    flops = 2 * 9 * channels * channels * pixels
    conv_cost = pl.CostEstimate(
        flops=flops, bytes_accessed=9 * channels * channels * 2 + 5 * channels * pixels * 2,
        transcendentals=channels * pixels,
    )
    tall = 2 * side + pixels
    conv_scratch = [VMEM((3, tall, channels), BF16)]
    plain = jax.ShapeDtypeStruct((pixels, channels), BF16)
    lined = jax.ShapeDtypeStruct((side + 1, micro, side, channels), BF16)
    tower = jax.ShapeDtypeStruct((micro, pixels, channels), F32)

    def forward(tick, arrays):
        return pl.pallas_call(
            functools.partial(forward_kernel, tick, side, micro),
            in_specs=[whole] * 6 + [far] * 2 if tick else [whole] * 4,
            out_specs=[whole, far, far, whole],
            out_shape=[plain, lined, tower, jax.ShapeDtypeStruct((8, 128), F32)],
            scratch_shapes=conv_scratch
            + [
                VMEM((side + 1, side, channels), BF16),
                VMEM((pixels, channels), F32),
                pltpu.SemaphoreType.DMA((2,)),
            ],
            input_output_aliases={6: 1, 7: 2} if tick else {},
            cost_estimate=conv_cost,
            compiler_params=params(),
            name="forward_conv",
        )(*arrays)

    def backward(tick, arrays):
        fixed = 4 + micro if tick else 2 + micro
        return pl.pallas_call(
            functools.partial(backward_kernel, tick, side, micro, norm_div),
            in_specs=[whole] * fixed + [far, whole] + [far] * (1 if tick else 0),
            out_specs=[whole, far],
            out_shape=[plain, lined],
            scratch_shapes=conv_scratch
            + [
                VMEM((pixels, channels), F32),
                VMEM((side + 1, side, channels), BF16),
                pltpu.SemaphoreType.DMA((2,)),
            ],
            input_output_aliases={fixed + 2: 1} if tick else {},
            cost_estimate=conv_cost,
            compiler_params=params(),
            name="backward_conv",
        )(*arrays)

    def moved(array, hops):
        apart = [[hop for hop in hops if min(hop) % 2 == odd] for odd in (0, 1)]
        chip = lax.ppermute(array, "section", apart[1]) if apart[1] else None
        core = lax.ppermute(array, "section", apart[0]) if apart[0] else chip
        return core, (core if chip is None else chip)

    scores = []
    kept_in = kept_conv = outgoing = None
    for tick in range(ticks):
        if tick:
            hops = [(i, i + 1) for i in range(sections - 1) if 0 <= tick - 1 - i < micro]
            arrays = (*moved(outgoing, hops), first_map, pack, head, flat_out, kept_in, kept_conv)
        else:
            arrays = (first_map, pack, head, flat_out)
        outgoing, kept_in, kept_conv, score = forward(tick, arrays)
        scores.append(score)
    scores = scores[sections - 1 :]
    for hop in range(sections - gen_count - 1):
        target = sections - 2 - hop
        passed = lax.ppermute(scores, "section", [(target + 1, target)])
        scores = [jnp.where(section_at == target, new, old) for new, old in zip(passed, scores)]

    mods = [kept_in]
    for flip in range(1, GROUP):
        mods.append(group_swap(kept_in, flip, sections, count))
    kept_grad = outgoing = None
    for tick in range(ticks):
        arrays = (head, pack, *scores, kept_conv, flat_out)
        if tick:
            hops = [(i, i - 1) for i in range(1, sections) if 0 <= tick - 1 - (sections - 1 - i) < micro]
            received = moved(outgoing, hops)
            arrays = (*received, *arrays, kept_grad)
        outgoing, kept_grad = backward(tick, arrays)

    part = channels // count
    own = channels // GROUP
    chunks = ((0, 1, 2, 3), (4, 5, 6), (7, 8))
    wide = micro * pixels + 128
    packed = pl.pallas_call(
        functools.partial(pack_kernel, micro, side, count),
        in_specs=[whole],
        out_specs=[whole] * GROUP,
        out_shape=[jax.ShapeDtypeStruct((own, wide), BF16)] * GROUP,
        scratch_shapes=[VMEM((channels, wide), BF16)],
        cost_estimate=pl.CostEstimate(flops=0, bytes_accessed=4 * micro * pixels * channels, transcendentals=0),
        compiler_params=params(),
        name="pack_grad",
    )(kept_grad)
    grads = [packed[0]]
    for flip in range(1, GROUP):
        grads.append(group_swap(packed[flip], flip, sections, count))
    slots = count // GROUP
    pieces = pl.pallas_call(
        functools.partial(shift_kernel, micro, side),
        in_specs=[whole] * GROUP,
        out_specs=whole,
        out_shape=jax.ShapeDtypeStruct((3, GROUP * micro * tall, channels), BF16),
        cost_estimate=pl.CostEstimate(flops=0, bytes_accessed=16 * 1024 * 1024, transcendentals=0),
        compiler_params=params(),
        name="shift",
    )(*mods)
    pairs = []
    for taps in chunks:
        pairs += pl.pallas_call(
            functools.partial(weight_grad_kernel, micro, side, count, taps),
            in_specs=[whole] * (2 * GROUP + 2),
            out_specs=[whole] * 2,
            out_shape=[
                jax.ShapeDtypeStruct((slots // 2, len(taps), part, channels), F32),
                jax.ShapeDtypeStruct((slots // 2, len(taps), part, channels), BF16),
            ],
            cost_estimate=pl.CostEstimate(
                flops=micro * flops // len(chunks), bytes_accessed=5 * 1024 * 1024, transcendentals=0
            ),
            compiler_params=params(),
            name="weight_grad",
        )(*grads, *mods, pieces, flat_out)
    done = [None] * 9
    for chunk, taps in enumerate(chunks):
        keep, send = pairs[2 * chunk], pairs[2 * chunk + 1]
        half = slots // 2
        while True:
            total = keep + group_swap(send, half << GROUP_BITS, sections, count).astype(F32)
            half //= 2
            if not half:
                break
            keep = total[:half]
            send = total[half:].astype(BF16)
        for spot, tap in enumerate(taps):
            done[tap] = total[0, spot]
    return jnp.stack(done, axis=1)[None]


def solution(mesh):
    placed = (
        P("dp", None),
        P("dp"),
        P("dp", None),
        P(),
        P(),
        P("section", None, None),
        P("section", None, None, None),
        P(),
    )
    return jax.shard_map(
        on_device,
        mesh=mesh,
        in_specs=placed,
        out_specs=P("section", "dp", None, None),
        check_vma=False,
    )
```

```python
import functools
import math

import jax
import jax.numpy as jnp
from jax import lax
from jax.experimental import pallas as pl
from jax.experimental.pallas import tpu as pltpu
from jax.sharding import PartitionSpec as P


TXT_LEN = 77
RES = 16
F32 = jnp.float32
BF16 = jnp.bfloat16
VMEM = pltpu.VMEM
LIMIT = 24 * 1024 * 1024


def params():
    return pltpu.CompilerParams(vmem_limit_bytes=LIMIT)


def swap(x, bit, count):
    return lax.ppermute(x, "dp", [(i, i ^ bit) for i in range(count)])


def device_flip(value, odd):
    if odd:
        return value
    low, high = value & 1, (value >> 2) & 1
    return (value & ~5) | (low << 2) | high


def own_flip(value, section):
    return jnp.where(section % 2 == 1, device_flip(value, 1), device_flip(value, 0))


def group_swap(x, value, sections, count, chosen=None):
    pairs = []
    for section in range(sections) if chosen is None else chosen:
        flip = device_flip(value, section % 2)
        pairs += [(section * count + i, section * count + (i ^ flip)) for i in range(count)]
    return lax.ppermute(x, ("section", "dp"), pairs)


def column_masks(rows, side):
    column = lax.broadcasted_iota(jnp.int32, (rows, 1), 0) % side
    return column != 0, column != side - 1


def put_shifts(pieces, value, side, at, rows):
    not_first, not_last = column_masks(rows, side)
    left = jnp.where(not_first, pltpu.roll(value, 1, 0), 0.0)
    right = jnp.where(not_last, pltpu.roll(value, rows - 1, 0), 0.0)
    for index, shifted in enumerate((left, value, right)):
        pieces[index, pl.ds(at, rows), :] = shifted.astype(BF16)


def blank_edges(pieces, rows, pad):
    blank = jnp.zeros((pad, pieces.shape[2]), BF16)
    for index in range(3):
        pieces[index, pl.ds(0, pad), :] = blank
        pieces[index, pl.ds(pad + rows, pad), :] = blank


def conv_of(pieces, weight, sign, side, rows):
    channels = pieces.shape[2]
    total = None
    for tap in range(9):
        down, across = sign * (tap // 3 - 1), sign * (tap % 3 - 1)
        term = lax.dot_general(
            pieces[across + 1, pl.ds(side + down * side, rows), :],
            weight[pl.ds(tap * channels, channels), :],
            (((1,), ((1 if sign > 0 else 0),)), ((), ())),
            preferred_element_type=F32,
        )
        total = term if total is None else total + term
    return total


def prepare_kernel(latent_in, weight, start, squares, first_map, latent):
    channels = weight.shape[1]
    latent[...] = latent_in[...]
    for block in range(0, channels, 64):
        total = None
        for tap in range(9):
            value = weight[pl.ds(tap * channels + block, 64), :].astype(F32)
            total = value * value if total is None else total + value * value
        squares[pl.ds(block, 64), :] = total
    first_map[...] = jnp.transpose(start[...].astype(F32)).astype(BF16)


def join_kernel(*refs):
    out = refs[-1]
    size = refs[0].shape[0]
    for index, ref in enumerate(refs[:-1]):
        out[pl.ds(index * size, size), :] = ref[...]


def text_kernel(ids, other_ids, table, stay, go):
    vocab_rows = table.shape[0]
    here = lax.axis_index("dp")
    half = ids.shape[0]
    full = vocab_rows // 128 * 128
    width = full if full == vocab_rows else full + 128
    row = lax.broadcasted_iota(jnp.int32, (2 * half, width), 1)
    row = jnp.where(row < vocab_rows, row + here * vocab_rows, -1)
    wanted = jnp.concatenate([ids[...], other_ids[...]], axis=0)
    hits = jnp.zeros((2 * half, width), F32)
    for token in range(TXT_LEN):
        hits = hits + jnp.where(wanted[:, token : token + 1] == row, 1.0, 0.0)
    hits = hits.astype(BF16)
    sums = jnp.dot(hits[:, :full], table[pl.ds(0, full), :], preferred_element_type=F32)
    if width > full:
        last = table[pl.ds(full, vocab_rows - full), :].astype(F32)
        blank = jnp.zeros((width - vocab_rows, table.shape[1]), F32)
        last = jnp.concatenate([last, blank], axis=0).astype(BF16)
        sums = sums + jnp.dot(hits[:, full:], last, preferred_element_type=F32)
    stay[...] = sums[:half]
    go[...] = sums[half:]


def add_kernel(one, two, *outs):
    total = one[...] + two[...]
    size = outs[0].shape[0]
    for index, out in enumerate(outs):
        out[...] = total[index * size : (index + 1) * size]


def style_kernel(*refs):
    sums, (latent, style_weight, squares, pack) = refs[:GROUP], refs[GROUP:]
    section = lax.axis_index("section")
    sections = lax.axis_size("section")
    is_gen = section < sections - sections // 4
    micro, channels = latent.shape
    text_mean = ((sums[0][...] + sums[1][...]) + (sums[2][...] + sums[3][...])) / TXT_LEN
    code = jnp.where(is_gen, latent[...] + text_mean, text_mean)
    code = jnp.concatenate([code, jnp.zeros((8 - micro, channels), F32)], axis=0).astype(BF16)
    across = (((1,), (1,)), ((), ()))
    styles = 1.0 + lax.dot_general(code, style_weight[...], across, preferred_element_type=F32)
    norms = lax.dot_general(
        styles * styles, squares[...], across, preferred_element_type=F32,
        precision=lax.Precision.HIGHEST,
    )
    pack[pl.ds(0, 8), :] = styles
    pack[pl.ds(8, 8), :] = jnp.where(is_gen, lax.rsqrt(norms + 1e-08), 1.0)


def forward_kernel(tick, side, micro, *refs):
    if tick:
        from_core, from_chip, start, pack, head, weight = refs[:6]
        refs = refs[8:]
    else:
        start, pack, head, weight = refs[:4]
        refs = refs[4:]
    out, kept_in, kept_conv, score, pieces, mod_box, conv_box, sems = refs
    rows = start.shape[0]
    section = lax.axis_index("section")
    position = tick - section

    @pl.when((position >= 0) & (position < micro))
    def _():
        blank_edges(pieces, rows, side)
        style = pack[pl.ds(position, 1), :]
        source = start[...].astype(F32)
        if tick:
            other = jnp.where(section % 2 == 1, from_core[...].astype(F32), from_chip[...].astype(F32))
            source = jnp.where(section == 0, source, other)
        mod = (style * source).astype(BF16)
        mod_box[pl.ds(0, side)] = mod.reshape(side, side, mod.shape[1])
        squared = style * style
        high = squared.astype(BF16).astype(F32)
        row = lax.broadcasted_iota(jnp.int32, (side, mod.shape[1]), 0)
        low = jnp.where(row < 4, squared - high, 0.0)
        mod_box[side] = jnp.where(row < 2, high, low).astype(BF16)
        first = pltpu.make_async_copy(mod_box, kept_in.at[:, position], sems.at[0])
        first.start()
        put_shifts(pieces, mod.astype(F32), side, side, rows)
        conv = conv_of(pieces, weight, 1, side, rows)
        conv_box[...] = conv
        second = pltpu.make_async_copy(conv_box, kept_conv.at[position], sems.at[1])
        second.start()
        pre = pack[pl.ds(8 + position, 1), :] * conv
        result = (pre / (1.0 + jnp.exp(-pre))).astype(BF16)
        out[...] = result
        sums = jnp.sum(result.astype(F32), axis=0, keepdims=True) * head[...]
        score[...] = jnp.broadcast_to(jnp.sum(sums, axis=1, keepdims=True), score.shape)
        first.wait()
        second.wait()


def backward_kernel(tick, side, micro, norm_div, *refs):
    if tick:
        from_core, from_chip = refs[:2]
        refs = refs[2:]
    head, pack = refs[:2]
    scores, refs = refs[2 : 2 + micro], refs[2 + micro :]
    kept_conv, weight = refs[:2]
    refs = refs[3:] if tick else refs[2:]
    out, kept_grad, pieces, conv_box, grad_box, sems = refs
    rows = conv_box.shape[0]
    section = lax.axis_index("section")
    sections = lax.axis_size("section")
    gen_count = sections - sections // 4
    position = tick - (sections - 1 - section)

    @pl.when((position >= 0) & (position < micro))
    def _():
        load = pltpu.make_async_copy(kept_conv.at[position], conv_box, sems.at[0])
        load.start()
        blank_edges(pieces, rows, side)
        raw = scores[0][...]
        for index in range(1, micro):
            raw = jnp.where(position == index, scores[index][...], raw)
        raw = raw[:1, :1] / norm_div
        d_factor = (1.0 / (1.0 + jnp.exp(-raw))).astype(BF16).astype(F32)
        g_factor = (-1.0 / (1.0 + jnp.exp(raw))).astype(BF16).astype(F32)
        scale = jnp.where(section < gen_count, jnp.ones_like(raw), d_factor)
        boost = jnp.where(section == gen_count, g_factor, jnp.ones_like(raw))
        demod = pack[pl.ds(8 + position, 1), :]
        unit = (head[...] / norm_div).astype(BF16).astype(F32)
        incoming = jnp.broadcast_to(unit, conv_box.shape)
        if tick:
            other = jnp.where(section % 2 == 0, from_core[...].astype(F32), from_chip[...].astype(F32))
            incoming = jnp.where(section == sections - 1, incoming, other)
        load.wait()
        conv = conv_box[...]
        pre = demod * conv
        sigma = 1.0 / (1.0 + jnp.exp(-pre))
        grad_pre = incoming * sigma * (1.0 + pre * (1.0 - sigma))
        grad_conv = demod * grad_pre
        channels = conv.shape[1]
        grad_box[pl.ds(0, side)] = (scale * grad_conv).astype(BF16).reshape(side, side, channels)
        term = jnp.sum(grad_pre * conv, axis=0, keepdims=True) * demod * demod * demod
        term = jnp.where(section < gen_count, term, 0.0)
        high = term.astype(BF16).astype(F32)
        row = lax.broadcasted_iota(jnp.int32, (side, channels), 0)
        both = jnp.where(row % 2 == 0, high, term - high)
        grad_box[side] = jnp.where(row < 4, both, 0.0).astype(BF16)
        first = pltpu.make_async_copy(grad_box, kept_grad.at[:, position], sems.at[1])
        first.start()
        put_shifts(pieces, grad_conv.astype(BF16).astype(F32), side, side, rows)
        back = conv_of(pieces, weight, -1, side, rows)
        out[...] = (pack[pl.ds(position, 1), :] * boost * back).astype(BF16)
        first.wait()


GROUP_BITS = 2
GROUP = 1 << GROUP_BITS


def pack_kernel(micro, side, count, kept_grad, *rest):
    outs, turned = rest[:GROUP], rest[GROUP]
    channels = kept_grad.shape[3]
    rows = side * micro * side
    part = channels // count
    here, section = lax.axis_index("dp"), lax.axis_index("section")
    extra = micro * side
    stacked = kept_grad[...].reshape(rows + extra, channels).astype(F32)
    stacked = jnp.concatenate([stacked, jnp.zeros((128 - extra, channels), F32)], axis=0)
    turned[...] = jnp.transpose(stacked).astype(BF16)
    for flip in range(GROUP):
        for slot in range(count // GROUP):
            block = here ^ own_flip(flip ^ (slot << GROUP_BITS), section)
            source = pl.multiple_of(block * part, part)
            outs[flip][pl.ds(slot * part, part), :] = turned[pl.ds(source, part), :]


def shift_kernel(micro, side, *refs):
    mods, (pieces, lines) = refs[: GROUP + 1], refs[GROUP + 1 :]
    channels = pieces.shape[2]
    rows = side * micro * side
    band = micro * side
    is_last = lax.axis_index("section") == lax.axis_size("section") - 1
    blank = jnp.zeros((band, channels), BF16)
    for member in range(GROUP):
        base = member * (rows + 2 * band)
        for index in range(3):
            pieces[index, pl.ds(base, band), :] = blank
            pieces[index, pl.ds(base + band + rows, band), :] = blank
        value = mods[member][...].reshape(rows + band, channels).astype(F32)
        if member == GROUP - 1:
            other = mods[GROUP][...].reshape(rows + band, channels).astype(F32)
            value = jnp.where(is_last, other, value)
        lines[pl.ds(member * 128, band), :] = value[rows:].astype(BF16)
        lines[pl.ds(member * 128 + band, 128 - band), :] = jnp.zeros((128 - band, channels), BF16)
        put_shifts(pieces, value[:rows], side, base + band, rows)


def weight_grad_kernel(micro, side, count, taps, *refs):
    grads, (pieces, lines, weight, keep, send) = refs[:GROUP], refs[GROUP:]
    channels = weight.shape[1]
    rows = side * micro * side
    band = micro * side
    tall = rows + 2 * band
    part = channels // count
    here, section = lax.axis_index("dp"), lax.axis_index("section")
    slots = count // GROUP
    mixture = None
    for member in range(GROUP):
        term = jnp.dot(
            grads[member][:, pl.ds(rows, 128)], lines[pl.ds(member * 128, 128), :],
            preferred_element_type=F32,
        )
        mixture = term if mixture is None else mixture + term
    for spot, tap in enumerate(taps):
        total = None
        for member in range(GROUP):
            begin = member * tall + (tap // 3) * band
            term = jnp.dot(
                grads[member][:, pl.ds(0, rows)], pieces[tap % 3, pl.ds(begin, rows), :],
                preferred_element_type=F32,
            )
            total = term if total is None else total + term
        for slot in range(slots):
            block = here ^ own_flip(slot << GROUP_BITS, section)
            source = pl.multiple_of(block * part, part)
            fixed = total[slot * part : (slot + 1) * part] - weight[
                pl.ds(tap * channels + source, part), :
            ].astype(F32) * mixture[slot * part : (slot + 1) * part]
            if slot < slots // 2:
                keep[slot, spot] = fixed
            else:
                send[slot - slots // 2, spot] = fixed.astype(BF16)


def final_kernel(first, keep, got, *refs):
    out, box, sems = refs[-3:]
    box[...] = keep[0] + got[0].astype(F32)
    copy = pltpu.make_async_copy(box, out.at[pl.ds(first, box.shape[0])], sems.at[0])
    copy.start()
    copy.wait()


def on_device(
    text_ids, seed_ids, text_table, latent_table, start_map, style_weight, conv_weight, score_head
):
    sections = lax.axis_size("section")
    count = lax.axis_size("dp")
    bits = count.bit_length() - 1
    gen_count = sections - sections // 4
    section_at = lax.axis_index("section")
    micro = seed_ids.shape[0]
    channels, pixels = start_map.shape
    side = RES
    norm_div = pixels * math.sqrt(channels)

    whole = pl.BlockSpec(memory_space=VMEM)
    far = pl.BlockSpec(memory_space=pltpu.HBM)
    flat_out = jnp.transpose(conv_weight[0], (1, 0, 2)).reshape(9 * channels, channels)

    def small(kernel, shapes, *arrays, specs=None, scratch=()):
        return pl.pallas_call(
            kernel,
            in_specs=specs or [whole] * len(arrays),
            out_specs=[whole] * len(shapes),
            out_shape=[jax.ShapeDtypeStruct(*shape) for shape in shapes],
            scratch_shapes=scratch,
            compiler_params=params(),
        )(*arrays)

    parts = [text_ids]
    for flip in range(1, GROUP):
        parts.append(swap(text_ids, flip, count))
    squares, first_map, latent = small(
        prepare_kernel,
        [((channels, channels), F32), ((pixels, channels), BF16), ((micro, channels), F32)],
        jnp.take(latent_table, seed_ids, axis=0), flat_out, start_map,
    )
    (ids,) = small(join_kernel, [((GROUP * micro, TXT_LEN), jnp.int32)], *parts)
    for stage in range(GROUP_BITS, bits):
        other_ids = swap(ids, 1 << stage, count)
        if stage < bits - 1:
            (ids,) = small(join_kernel, [((2 * ids.shape[0], TXT_LEN), jnp.int32)], ids, other_ids)
    half = count * micro // 2
    stay, go = small(text_kernel, [((half, channels), F32)] * 2, ids, other_ids, text_table)
    for stage in reversed(range(GROUP_BITS, bits)):
        got = swap(go, 1 << stage, count)
        size, outs = (micro, GROUP) if stage == GROUP_BITS else (half // 2, 2)
        sums = small(add_kernel, [((size, channels), F32)] * outs, stay, got)
        if stage > GROUP_BITS:
            stay, go = sums
            half //= 2
    sums = list(sums)
    for flip in range(1, GROUP):
        sums[flip] = swap(sums[flip], flip, count)
    (pack,) = small(style_kernel, [((16, channels), F32)], *sums, latent, style_weight[0], squares)
    head = score_head[None]
    ticks = micro + sections - 1

    flops = 2 * 9 * channels * channels * pixels
    conv_cost = pl.CostEstimate(
        flops=flops, bytes_accessed=9 * channels * channels * 2 + 5 * channels * pixels * 2,
        transcendentals=channels * pixels,
    )
    tall = 2 * side + pixels
    conv_scratch = [VMEM((3, tall, channels), BF16)]
    plain = jax.ShapeDtypeStruct((pixels, channels), BF16)
    lined = jax.ShapeDtypeStruct((side + 1, micro, side, channels), BF16)
    tower = jax.ShapeDtypeStruct((micro, pixels, channels), F32)

    def forward(tick, arrays):
        return pl.pallas_call(
            functools.partial(forward_kernel, tick, side, micro),
            in_specs=[whole] * 6 + [far] * 2 if tick else [whole] * 4,
            out_specs=[whole, far, far, whole],
            out_shape=[plain, lined, tower, jax.ShapeDtypeStruct((8, 128), F32)],
            scratch_shapes=conv_scratch
            + [
                VMEM((side + 1, side, channels), BF16),
                VMEM((pixels, channels), F32),
                pltpu.SemaphoreType.DMA((2,)),
            ],
            input_output_aliases={6: 1, 7: 2} if tick else {},
            cost_estimate=conv_cost,
            compiler_params=params(),
            name="forward_conv",
        )(*arrays)

    def backward(tick, arrays):
        fixed = 4 + micro if tick else 2 + micro
        return pl.pallas_call(
            functools.partial(backward_kernel, tick, side, micro, norm_div),
            in_specs=[whole] * fixed + [far, whole] + [far] * (1 if tick else 0),
            out_specs=[whole, far],
            out_shape=[plain, lined],
            scratch_shapes=conv_scratch
            + [
                VMEM((pixels, channels), F32),
                VMEM((side + 1, side, channels), BF16),
                pltpu.SemaphoreType.DMA((2,)),
            ],
            input_output_aliases={fixed + 2: 1} if tick else {},
            cost_estimate=conv_cost,
            compiler_params=params(),
            name="backward_conv",
        )(*arrays)

    def moved(array, hops):
        apart = [[hop for hop in hops if min(hop) % 2 == odd] for odd in (0, 1)]
        chip = lax.ppermute(array, "section", apart[1]) if apart[1] else None
        core = lax.ppermute(array, "section", apart[0]) if apart[0] else chip
        return core, (core if chip is None else chip)

    scores = []
    kept_in = kept_conv = outgoing = None
    for tick in range(ticks):
        if tick:
            hops = [(i, i + 1) for i in range(sections - 1) if 0 <= tick - 1 - i < micro]
            arrays = (*moved(outgoing, hops), first_map, pack, head, flat_out, kept_in, kept_conv)
        else:
            arrays = (first_map, pack, head, flat_out)
        outgoing, kept_in, kept_conv, score = forward(tick, arrays)
        scores.append(score)
    scores = scores[sections - 1 :]
    for hop in range(sections - gen_count - 1):
        target = sections - 2 - hop
        passed = lax.ppermute(scores, "section", [(target + 1, target)])
        scores = [jnp.where(section_at == target, new, old) for new, old in zip(passed, scores)]

    mods = [kept_in]
    for flip in (1, 2):
        mods.append(group_swap(kept_in, flip, sections, count))
    mods.append(group_swap(kept_in, 3, sections, count, range(sections - 1)))
    mods.append(group_swap(mods[2], 1, sections, count, (sections - 1,)))
    kept_grad = outgoing = None
    for tick in range(ticks):
        arrays = (head, pack, *scores, kept_conv, flat_out)
        if tick:
            hops = [(i, i - 1) for i in range(1, sections) if 0 <= tick - 1 - (sections - 1 - i) < micro]
            received = moved(outgoing, hops)
            arrays = (*received, *arrays, kept_grad)
        outgoing, kept_grad = backward(tick, arrays)

    part = channels // count
    own = channels // GROUP
    chunks = ((0, 1, 2, 3), (4, 5, 6), (7, 8))
    wide = micro * pixels + 128
    packed = pl.pallas_call(
        functools.partial(pack_kernel, micro, side, count),
        in_specs=[whole],
        out_specs=[whole] * GROUP,
        out_shape=[jax.ShapeDtypeStruct((own, wide), BF16)] * GROUP,
        scratch_shapes=[VMEM((channels, wide), BF16)],
        cost_estimate=pl.CostEstimate(flops=0, bytes_accessed=4 * micro * pixels * channels, transcendentals=0),
        compiler_params=params(),
        name="pack_grad",
    )(kept_grad)
    grads = [packed[0]]
    for flip in range(1, GROUP):
        grads.append(group_swap(packed[flip], flip, sections, count))
    slots = count // GROUP
    pieces, lines = pl.pallas_call(
        functools.partial(shift_kernel, micro, side),
        in_specs=[whole] * (GROUP + 1),
        out_specs=[whole] * 2,
        out_shape=[
            jax.ShapeDtypeStruct((3, GROUP * micro * tall, channels), BF16),
            jax.ShapeDtypeStruct((GROUP * 128, channels), BF16),
        ],
        cost_estimate=pl.CostEstimate(flops=0, bytes_accessed=16 * 1024 * 1024, transcendentals=0),
        compiler_params=params(),
        name="shift",
    )(*mods)
    pairs = []
    for taps in chunks:
        called = pl.pallas_call(
            functools.partial(weight_grad_kernel, micro, side, count, taps),
            in_specs=[whole] * (GROUP + 3),
            out_specs=[whole] * 2,
            out_shape=[
                jax.ShapeDtypeStruct((slots // 2, len(taps), part, channels), F32),
                jax.ShapeDtypeStruct((slots // 2, len(taps), part, channels), BF16),
            ],
            cost_estimate=pl.CostEstimate(
                flops=micro * flops // len(chunks), bytes_accessed=5 * 1024 * 1024, transcendentals=0
            ),
            compiler_params=params(),
            name="weight_grad",
        )
        pairs += called(*grads, pieces, lines, flat_out)
    result = ()
    for chunk, taps in enumerate(chunks):
        keep, send = pairs[2 * chunk], pairs[2 * chunk + 1]
        half = slots // 2
        while True:
            got = group_swap(send, half << GROUP_BITS, sections, count)
            half //= 2
            if not half:
                break
            total = keep + got.astype(F32)
            keep = total[:half]
            send = total[half:].astype(BF16)
        result = pl.pallas_call(
            functools.partial(final_kernel, taps[0]),
            in_specs=[whole, whole] + [far] * len(result),
            out_specs=[far],
            out_shape=[jax.ShapeDtypeStruct((9, part, channels), F32)],
            scratch_shapes=[VMEM((len(taps), part, channels), F32), pltpu.SemaphoreType.DMA((1,))],
            input_output_aliases={2: 0} if result else {},
            compiler_params=params(),
            name="final",
        )(keep, got, *result)
    return jnp.transpose(result[0], (1, 0, 2))[None]


def solution(mesh):
    placed = (
        P("dp", None),
        P("dp"),
        P("dp", None),
        P(),
        P(),
        P("section", None, None),
        P("section", None, None, None),
        P(),
    )
    return jax.shard_map(
        on_device,
        mesh=mesh,
        in_specs=placed,
        out_specs=P("section", "dp", None, None),
        check_vma=False,
    )
```
